32 devices in a mesh: pair: 2 (over x), grow: 4 (over y, core), gcol: 4 (over z).
Axes of the slice: x: 2, y: 2, z: 4, core: 2. Of those that a mesh axis runs over, the one named last changes fastest.
Arguments:
- core_matrix: bfloat16 [12288, 12288], P('grow', 'gcol'), may hold values from -0.00048828125 to 0.00048828125
- pair_panels: bfloat16 [12, 32, 12288], P('pair', None, ('grow', 'gcol')), may hold values from -6 to 6
- amplitudes: bfloat16 [12, 32, 32], P('pair'), may hold values from -0.1875 to 0.1875
- pair_widths: int32 [12], P('pair'), may hold values from 8 to 32
- batch_plan: int32 [12], P('pair'), may hold values from 0 to 11, each once
Outputs:
- residual: float32 [12, 1024], P('pair', ('grow', 'gcol'))
The draws below stay inside these ranges and needn't reach their ends.
Inputs may be any that keep to these rules, and one draw needn't show every extreme that they name: batch_plan names every pair exactly once.
All inputs are finite; a program needn't handle non-finite values.
Results may differ from the reference program's by a relative error of at most 0.015.
Values may be sent and summed in bfloat16 or wider, within the bound.
A program may use at most 64 MiB of HBM per device.

```python
import jax
import jax.numpy as jnp
from jax import lax

NG = 12288
NPNO = 32
PAIRS = 12


def set_ends(drawn, key, low, top_value):
    longest = drawn.shape.index(max(drawn.shape))
    spots = []
    for shift in (0, 1):
        where = [jax.random.randint(jax.random.fold_in(key, axis), (), 0, length) for axis, length in enumerate(drawn.shape)]
        where[longest] = (where[longest] + shift) % drawn.shape[longest]
        spots.append(tuple(where))
    return drawn.at[spots[0]].set(low).at[spots[1]].set(top_value)


def shard_levels(rng, dims, split, smallest, high):
    factor_of = 1.0
    for axis_at, shards_of in split:
        draws = jax.random.uniform(jax.random.fold_in(jax.random.fold_in(rng, 6), axis_at), (shards_of,), jnp.float32, smallest / len(split), high / len(split))
        factor_of = factor_of * jnp.repeat(jnp.exp(draws), dims[axis_at] // shards_of).reshape((-1,) + (1,) * (len(dims) - 1 - axis_at))
    return factor_of


def gaussian(own_key, shape, scale, reach, shards=(), kind=jnp.bfloat16):
    drawn = scale * jax.random.normal(own_key, shape, jnp.float32)
    if shards:
        drawn = drawn * shard_levels(own_key, shape, shards, -0.22, 0.18)
    return jnp.clip(drawn, -reach, reach).astype(kind)


def setup_inputs(seed: int = 0) -> dict:
    splits = jax.random.split(jax.random.key(seed), 6)
    return {
        "core_matrix": gaussian(splits[0], (NG, NG), (NG * NG) ** -0.5, 0.00048828125, ((0, 4), (1, 4))),
        "pair_panels": gaussian(splits[1], (PAIRS, NPNO, NG), 1.0, 6.0, ((0, 2), (2, 16))),
        "amplitudes": gaussian(splits[2], (PAIRS, NPNO, NPNO), (NPNO * NPNO) ** -0.5, 0.1875, ((0, 2),)),
        "pair_widths": set_ends(jax.random.randint(splits[3], (PAIRS,), NPNO // 4, NPNO + 1), jax.random.fold_in(splits[3], 1), NPNO // 4, NPNO).astype(jnp.int32),
        "batch_plan": jax.random.permutation(splits[4], PAIRS).astype(jnp.int32),
    }


def pair_term(core_matrix, panel, amps, width):
    live = (lax.iota(jnp.int32, NPNO) < width).astype(jnp.bfloat16)
    masked = amps * live[:, None] * live[None, :]
    projected = jnp.dot(masked, panel, preferred_element_type=jnp.float32).astype(jnp.bfloat16)
    block = min(512, NG)
    count = NG // block

    def step(total, which):
        start = (which * block).astype(jnp.int32)
        left = lax.dynamic_slice_in_dim(panel, start, block, 1)
        core_rows = lax.dynamic_slice_in_dim(core_matrix, start, block, 0)
        coupled = lax.dot_general(left, projected, (((0,), (0,)), ((), ())), preferred_element_type=jnp.float32).astype(jnp.bfloat16)
        coupled = lax.optimization_barrier(coupled)
        weighted = (core_rows.astype(jnp.float32) * coupled.astype(jnp.float32)).astype(jnp.bfloat16)
        back = lax.dot_general(weighted, panel, (((1,), (1,)), ((), ())), preferred_element_type=jnp.float32).astype(jnp.bfloat16)
        total = total + jnp.dot(left, back, preferred_element_type=jnp.float32)
        return total, None

    total, _ = lax.scan(step, jnp.zeros((NPNO, NPNO), jnp.float32), jnp.arange(count, dtype=jnp.int32))
    keep = live.astype(jnp.float32)
    return (total * keep[:, None] * keep[None, :]).reshape(NPNO * NPNO)


def reference(core_matrix, pair_panels, amplitudes, pair_widths, batch_plan):
    def single(pair_id):
        return pair_term(core_matrix, pair_panels[pair_id], amplitudes[pair_id], pair_widths[pair_id])

    return lax.map(single, batch_plan)
```

```python
import functools

import jax
import jax.numpy as jnp
from jax import lax
from jax.experimental import pallas as pl
from jax.experimental.pallas import tpu as pltpu
from jax.sharding import PartitionSpec as P

MESH = pl.DeviceIdType.MESH
TILE = 1024
F32 = jnp.float32
BF16 = jnp.bfloat16
GROUP = 8
STATIC = 16


def units():
    found = []
    for high in range(STATIC // GROUP):
        for low in range(high + 1):
            for turn in range(GROUP // 2 + 1 if low == high else GROUP):
                found.append((high, low, turn, high != low or turn % (GROUP // 2) != 0))
    return found


def turned(block, turn):
    return block if turn % GROUP == 0 else pltpu.roll(block, turn % GROUP, 0)


def static_kernel(
        ngrow, ngcol, step, widths, panel_ref, amps_ref, core_ref, left_ref, right_ref, proj_ref, back_ref,
        z_ref, y_ref, v_ref, mix_ref, send_sem, recv_sem, tree_send, tree_recv, own_sem, z_sem):
    x, g, c = lax.axis_index("pair"), lax.axis_index("grow"), lax.axis_index("gcol")
    npair, depth, piece = panel_ref.shape
    half = depth // 2
    cols = core_ref.shape[1]
    steps = cols // step
    per = len(units()) * GROUP
    bits = ngrow.bit_length() - 1
    root = lax.div(c * ngrow, ngcol)
    first = lax.rem(c * ngrow, ngcol)

    def bit(value, b):
        return lax.rem(lax.div(value, 1 << b), 2)

    def flip(b):
        return g + (1 << b) * (1 - 2 * bit(g, b))

    differ = [lax.rem(bit(g, b) + bit(root, b), 2) for b in range(bits)]
    before = [jnp.int32(0)]
    for b in range(bits):
        before.append(before[-1] + differ[b])
    is_root = before[bits] == 0

    def order(t):
        both = jnp.minimum(c, ngcol - 1 - c)
        near = lax.div(t + 1, 2)
        inner = c + near * (1 - 2 * lax.rem(t, 2))
        outer = jnp.where(c < ngcol - 1 - c, c + t - both, c - t + both)
        return jnp.where(t <= 2 * both, inner, outer)

    def core_copy(t):
        rows = pl.ds(pl.multiple_of(order(t) * piece, 128), piece)
        return pltpu.make_async_copy(core_ref.at[rows, :], z_ref.at[rows, :], z_sem.at[t])

    for t in range(ngcol):
        core_copy(t).start()

    barrier = pltpu.get_barrier_semaphore()

    def greet(device):
        pl.semaphore_signal(barrier, inc=1, device_id=device, device_id_type=MESH)

    expected = jnp.int32(0)
    for far in (1, 2):
        for way in (0, 1):
            other = c + far * (1 - 2 * way)
            there = jnp.logical_and(other >= 0, other < ngcol)
            expected += jnp.where(there, 1, 0)

            @pl.when(there)
            def _(other=other):
                greet((x, g, other))

    for b in range(bits):
        expected += jnp.where(before[b] == 0, 1, 0)

        @pl.when(before[b] == 0)
        def _(b=b):
            greet((x, flip(b), c))

    def clear(i, carry):
        v_ref[pl.ds(pl.multiple_of(i * per, GROUP), per), :] = jnp.zeros((per, cols), F32)
        return carry

    lax.fori_loop(0, npair, clear, 0)
    left_ref[:, :, pl.ds(pl.multiple_of(c * piece, 128), piece)] = panel_ref[...]

    def span(at):
        return pl.ds(pl.multiple_of(at * piece, 128), piece)

    def build(at):
        def one(p, carry):
            rows = left_ref[p, 0:STATIC, span(at)].astype(F32)
            block = [rows[GROUP * k : GROUP * (k + 1)] for k in range(STATIC // GROUP)]
            made = [block[high] * turned(block[low], -turn) for high, low, turn, _ in units()]
            for k in range(0, len(made), 2):
                both = jnp.concatenate(made[k : k + 2], axis=0).astype(BF16)
                y_ref[pl.ds(pl.multiple_of(p * per + GROUP * k, 16), 16), :] = both
            return carry

        lax.fori_loop(0, npair, one, 0)

    build(c)

    whole = npair * depth
    pick_row = lax.broadcasted_iota(jnp.int32, (depth, whole), 0)
    pick_col = lax.broadcasted_iota(jnp.int32, (depth, whole), 1)
    pick = jnp.where(lax.rem(pick_col, depth) == pick_row, 1.0, 0.0).astype(BF16)
    row = lax.broadcasted_iota(jnp.int32, (whole, whole), 0)
    col = lax.broadcasted_iota(jnp.int32, (whole, whole), 1)
    width = jnp.zeros((whole, whole), jnp.int32)
    for p in range(npair):
        width = jnp.where(lax.div(row, depth) == p, widths[p], width)
    keep = jnp.logical_and(lax.div(row, depth) == lax.div(col, depth), jnp.logical_and(lax.rem(row, depth) < width, lax.rem(col, depth) < width))
    spread = jnp.dot(amps_ref[...].reshape(whole, depth), pick, preferred_element_type=F32)
    mix_ref[...] = jnp.where(keep, spread, 0.0).astype(BF16)

    pl.semaphore_wait(barrier, expected)

    def spot(ref, h, at):
        return ref.at[:, h * half : (h + 1) * half, span(at)]

    def hop(h, at, far, way, own):
        return pltpu.make_async_remote_copy(
            src_ref=panel_ref.at[:, h * half : (h + 1) * half, :] if own else spot(left_ref, h, at), dst_ref=spot(left_ref, h, at),
            send_sem=send_sem.at[h, at, far - 1, way], recv_sem=recv_sem.at[h, at],
            device_id=(x, g, c + far * (1 - 2 * way)), device_id_type=MESH)

    def branch(b, h, j, at):
        return pltpu.make_async_remote_copy(
            src_ref=spot(right_ref, h, j) if at is None else spot(left_ref, h, at), dst_ref=spot(right_ref, h, j),
            send_sem=tree_send.at[b, h, j], recv_sem=tree_recv.at[h, j],
            device_id=(x, flip(b), c), device_id_type=MESH)

    def own_right(h, j, at):
        return pltpu.make_async_copy(spot(left_ref, h, at), spot(right_ref, h, j), own_sem.at[h, j])

    def arrivals(s):
        return [(c - s, 0, c - s >= 0)] if s == 0 else [(c - s, 0, c - s >= 0), (c + s, 1, c + s <= ngcol - 1)]

    def inside(at):
        return jnp.logical_and(at >= first, at < first + ngrow)

    def onward(h, far, s, act):
        ways = [(c, 0, c >= 0), (c, 1, c >= 0)] if s == 0 else arrivals(s)
        for at, way, valid in ways:
            other = c + far * (1 - 2 * way)

            @pl.when(jnp.logical_and(valid, jnp.logical_and(other >= 0, other < ngcol)))
            def _(at=at, way=way):
                act(hop(h, at, far, way, s == 0))

    def start(copy):
        copy.start()

    def wait_send(copy):
        copy.wait_send()

    def to_tree(h, s):
        for at, _, valid in arrivals(s):
            @pl.when(jnp.logical_and(is_root, jnp.logical_and(valid, inside(at))))
            def _(at=at):
                for b in reversed(range(bits)):
                    branch(b, h, at - first, at).start()
                own_right(h, at - first, at).start()

    def take(h, s):
        for at, _, valid in arrivals(s):
            @pl.when(valid)
            def _(at=at):
                hop(h, at, 1, 0, False).wait_recv()

        if s % 2 == 0:
            onward(h, 1, s, start)
            if h == 1:
                onward(h, 2, s, start)
        to_tree(h, s)
        if h == 0 and s % 2 == 0:
            onward(h, 2, s, start)
        if h == 0 and s == 2:
            onward(1, 2, 0, start)

    def tree(h, s):
        for at, _, valid in arrivals(s):
            here = jnp.logical_and(valid, inside(at))

            @pl.when(jnp.logical_and(is_root, here))
            def _(at=at):
                own_right(h, at - first, at).wait()

            @pl.when(jnp.logical_and(jnp.logical_not(is_root), here))
            def _(at=at):
                branch(0, h, at - first, None).wait_recv()
                for b in range(bits):
                    @pl.when(before[b + 1] == 0)
                    def _(b=b):
                        branch(b, h, at - first, None).start()

    onward(0, 1, 0, start)
    onward(0, 2, 0, start)
    onward(1, 1, 0, start)
    to_tree(0, 0)
    to_tree(1, 0)

    plan = {}
    for t in range(1, ngcol - 1):
        plan.setdefault(t * steps, []).append((take, 0, t))
        plan.setdefault(t * steps + steps // 2, []).extend([(tree, 0, t - 1)] + ([(tree, 1, 0)] if t == 1 else [(take, 1, t - 1)]))

    def gain(i, t, s):
        wide = pl.ds(pl.multiple_of(s * step, 128), step)
        v_ref[:, wide] += jnp.dot(y_ref[...], z_ref[span(order(t)), wide], preferred_element_type=F32)

    def early(i, carry):
        t, s = lax.div(i, steps), lax.rem(i, steps)
        for when, jobs in plan.items():
            @pl.when(i == when)
            def _(jobs=jobs):
                for job, h, distance in jobs:
                    job(h, distance)

        for k in range(ngcol - 1):
            @pl.when(i == k * steps)
            def _(k=k):
                core_copy(k).wait()

        @pl.when(jnp.logical_and(s == 0, t > 0))
        def _():
            build(order(t))

        gain(i, t, s)
        return carry

    lax.fori_loop(0, (ngcol - 1) * steps, early, 0)

    take(0, ngcol - 1)
    last = ngcol - 1
    build(order(last))
    core_copy(last).wait()

    def fold(wide):
        def one(p, carry):
            proj = proj_ref[pl.ds(pl.multiple_of(p * depth, depth), STATIC), wide].astype(F32)
            block = [proj[GROUP * k : GROUP * (k + 1)] for k in range(STATIC // GROUP)]
            total = [None] * len(block)
            for k, (high, low, turn, both) in enumerate(units()):
                v = v_ref[pl.ds(pl.multiple_of(p * per, GROUP) + GROUP * k, GROUP), wide]
                straight = v * turned(block[low], -turn)
                total[high] = straight if total[high] is None else total[high] + straight
                if both:
                    cross = turned(v * block[high], turn)
                    total[low] = cross if total[low] is None else total[low] + cross
            for k, value in enumerate(total):
                back_ref[pl.ds(pl.multiple_of(p * STATIC, STATIC) + GROUP * k, GROUP), wide] = value
            return carry

        lax.fori_loop(0, npair, one, 0)

    def late(k):
        at = order(k)

        @pl.when(inside(at))
        def _():
            here = span(at - first)
            right = right_ref[:, :, here].reshape(whole, piece)
            proj_ref[:, here] = jnp.dot(mix_ref[...], right, preferred_element_type=F32).astype(BF16)

            def one(s, carry):
                wide = pl.ds(pl.multiple_of((at - first) * piece + s * step, 128), step)
                v_ref[:, wide] += jnp.dot(y_ref[...], z_ref[span(order(last)), wide], preferred_element_type=F32)
                fold(wide)
                return carry

            lax.fori_loop(0, piece // step, one, 0)

    for k in range(ngcol):
        if k == 0 and ngcol == 2:
            take(1, 1)
        if 1 <= k < ngcol - 1 and k + 1 >= ngcol - 2:
            take(1, k + 1)
        if k >= ngcol - 2:
            tree(0, k)
        if k >= 1:
            tree(1, k)
        late(k)

    for h in (0, 1):
        for s in range(0, ngcol, 2):
            onward(h, 1, s, wait_send)
            onward(h, 2, s, wait_send)
        for s in range(ngcol):
            for at, _, valid in arrivals(s):
                here = jnp.logical_and(valid, inside(at))
                for b in range(bits):
                    @pl.when(jnp.logical_and(before[b + 1] == 0, here))
                    def _(at=at, b=b):
                        branch(b, h, at - first, None).wait_send()


def static_part(panels, amplitudes, widths, core_matrix, ngrow, ngcol):
    npair, depth, piece = panels.shape
    rows, cols = core_matrix.shape
    step = 256 if piece % 256 == 0 else 128
    made = npair * len(units()) * GROUP
    bits = ngrow.bit_length() - 1
    vmem = pl.BlockSpec(memory_space=pltpu.VMEM)
    return pl.pallas_call(
        functools.partial(static_kernel, ngrow, ngcol, step),
        out_shape=(
            jax.ShapeDtypeStruct((npair, depth, rows), BF16),
            jax.ShapeDtypeStruct((npair, depth, cols), BF16),
            jax.ShapeDtypeStruct((npair * depth, cols), BF16),
            jax.ShapeDtypeStruct((npair * STATIC, cols), F32),
        ),
        in_specs=[pl.BlockSpec(memory_space=pltpu.SMEM), vmem, vmem, pl.BlockSpec(memory_space=pl.ANY)],
        out_specs=[vmem] * 4,
        scratch_shapes=[
            pltpu.VMEM((rows, cols), BF16),
            pltpu.VMEM((made, piece), BF16),
            pltpu.VMEM((made, cols), F32),
            pltpu.VMEM((npair * depth, npair * depth), BF16),
            pltpu.SemaphoreType.DMA((2, ngcol, 2, 2)),
            pltpu.SemaphoreType.DMA((2, ngcol)),
            pltpu.SemaphoreType.DMA((bits, 2, ngrow)),
            pltpu.SemaphoreType.DMA((2, ngrow)),
            pltpu.SemaphoreType.DMA((2, ngrow)),
            pltpu.SemaphoreType.DMA((ngcol,)),
        ],
        compiler_params=pltpu.CompilerParams(collective_id=0, has_side_effects=True, vmem_limit_bytes=48 << 20),
        name="static_part",
    )(widths, panels, amplitudes, core_matrix)


def rest_kernel(widths, left_ref, right_ref, proj_ref, back_ref, core_ref, out_ref, z_ref, y_ref, x_ref, v_ref, p_ref, g_ref, sum_ref, lad_ref, z_sem):
    npair, depth, rows = left_ref.shape
    cols = core_ref.shape[1]
    tile = v_ref.shape[1]
    whole = npair * depth
    groups = depth // GROUP
    skip = STATIC // GROUP

    def core_copy(j):
        lanes = pl.ds(j * tile, tile)
        return pltpu.make_async_copy(core_ref.at[:, lanes], z_ref.at[j], z_sem.at[j])

    for j in range(cols // tile):
        core_copy(j).start()

    def duos(p):
        return lax.div(widths[p] + 1, 2)

    def rows_in(p):
        count = duos(p)
        found = jnp.int32(0)
        for group in range(skip, groups):
            found += 16 * (group + 1) * jnp.clip(count - 4 * group, 0, 4)
        return found

    def each_duo(p, offset, body):
        count = duos(p)
        for group in range(skip, groups):
            low = 4 * group
            begin = offset

            def run(duo, carry, group=group, low=low, begin=begin):
                body(group, 2 * duo, pl.multiple_of(begin + 16 * (group + 1) * (duo - low), 16))
                return carry

            lax.fori_loop(low, jnp.clip(count, low, low + 4), run, 0)
            offset = offset + 16 * (group + 1) * jnp.clip(count - low, 0, 4)

    def build(p, offset):
        x_ref[...] = left_ref[p].astype(F32)

        def duo(group, a, base):
            first, second = x_ref[pl.ds(a, 1), :], x_ref[pl.ds(a + 1, 1), :]
            for other in range(group + 1):
                block = x_ref[GROUP * other : GROUP * (other + 1), :]
                both = jnp.concatenate([first * block, second * block], axis=0)
                y_ref[pl.ds(base + 16 * other, 16), :] = both.astype(BF16)

        each_duo(p, offset, duo)
        return offset + rows_in(p)

    total = lax.fori_loop(0, npair, build, jnp.int32(0))
    sum_ref[...] = jnp.zeros_like(sum_ref)
    sizes = (512, 256, 128)

    for j in range(cols // tile):
        core_copy(j).wait()
        lanes = slice(j * tile, (j + 1) * tile)

        def multiply(size, base, i, carry):
            at = pl.ds(pl.multiple_of(base + i * size, 128), size)
            v_ref[at, :] = jnp.dot(y_ref[at, :], z_ref[j], preferred_element_type=F32)
            return carry

        done = jnp.int32(0)
        for size in sizes:
            count = lax.div(total - done + (0 if size > sizes[-1] else size - 1), size)
            lax.fori_loop(0, count, functools.partial(multiply, size, done), 0)
            done = done + count * size

        def fold(p, offset):
            mine = pl.ds(pl.multiple_of(p * depth, depth), depth)
            low = pl.ds(pl.multiple_of(p * depth, depth), STATIC)
            high = pl.ds(pl.multiple_of(p * depth, depth) + STATIC, depth - STATIC)
            p_ref[...] = proj_ref[mine, lanes].astype(F32)
            g_ref[low, :] = back_ref[pl.ds(pl.multiple_of(p * STATIC, STATIC), STATIC), lanes]
            g_ref[high, :] = jnp.zeros((depth - STATIC, tile), F32)
            origin = p * depth

            def duo(group, a, base):
                first, second = p_ref[pl.ds(a, 1), :], p_ref[pl.ds(a + 1, 1), :]
                sum0 = sum1 = None
                for other in range(group + 1):
                    upper = v_ref[pl.ds(base + 16 * other, 8), :]
                    lower = v_ref[pl.ds(base + 16 * other + 8, 8), :]
                    proj = p_ref[GROUP * other : GROUP * (other + 1), :]
                    sum0 = upper * proj if sum0 is None else sum0 + upper * proj
                    sum1 = lower * proj if sum1 is None else sum1 + lower * proj
                    if other < group:
                        g_ref[pl.ds(pl.multiple_of(origin, depth) + GROUP * other, GROUP), :] += upper * first + lower * second
                g_ref[pl.ds(origin + a, 1), :] += jnp.sum(sum0, axis=0, keepdims=True)
                g_ref[pl.ds(origin + a + 1, 1), :] += jnp.sum(sum1, axis=0, keepdims=True)

            each_duo(p, offset, duo)
            return offset + rows_in(p)

        lax.fori_loop(0, npair, fold, jnp.int32(0))
        sum_ref[...] += lax.dot_general(
            g_ref[...].astype(BF16), right_ref[:, :, lanes].reshape(whole, tile), (((1,), (1,)), ((), ())), preferred_element_type=F32)

    out_ref[...] = jnp.zeros_like(out_ref)
    ngrow, ngcol, padded, lanes = out_ref.shape
    share = depth // (ngrow * ngcol)
    for p in range(npair):
        width = widths[p]
        live = jnp.logical_and(
            lax.broadcasted_iota(jnp.int32, (depth, depth), 0) < width,
            lax.broadcasted_iota(jnp.int32, (depth, depth), 1) < width)
        lad_ref[...] = jnp.where(live, sum_ref[depth * p : depth * (p + 1), depth * p : depth * (p + 1)], 0.0)
        parts = [lad_ref[pl.ds(r, ngrow * ngcol, stride=share), :] for r in range(share)]
        row = parts[0] if share == 1 else jnp.concatenate(parts, axis=1)
        for at in range(ngrow):
            out_ref[at, :, p, 0 : share * depth] = row[at * ngcol : (at + 1) * ngcol]


def rest(left, right, proj, back, widths, core_matrix, ngrow, ngcol):
    npair, depth, rows = left.shape
    cols = core_matrix.shape[1]
    tile = TILE if cols % TILE == 0 else cols // 2
    most = npair * sum(16 * (group + 1) * 4 for group in range(STATIC // GROUP, depth // GROUP))
    most = -(-most // 128) * 128
    padded = -(-npair // 8) * 8
    vmem = pl.BlockSpec(memory_space=pltpu.VMEM)
    return pl.pallas_call(
        rest_kernel,
        out_shape=jax.ShapeDtypeStruct((ngrow, ngcol, padded, 128), F32),
        in_specs=[pl.BlockSpec(memory_space=pltpu.SMEM)] + [vmem] * 4 + [pl.BlockSpec(memory_space=pl.ANY)],
        out_specs=vmem,
        scratch_shapes=[
            pltpu.VMEM((cols // tile, rows, tile), BF16),
            pltpu.VMEM((most, rows), BF16),
            pltpu.VMEM((depth, rows), F32),
            pltpu.VMEM((most, tile), F32),
            pltpu.VMEM((depth, tile), F32),
            pltpu.VMEM((npair * depth, tile), F32),
            pltpu.VMEM((npair * depth, npair * depth), F32),
            pltpu.VMEM((depth, depth), F32),
            pltpu.SemaphoreType.DMA((cols // tile,)),
        ],
        compiler_params=pltpu.CompilerParams(vmem_limit_bytes=58 << 20),
        name="rest",
    )(widths, left, right, proj, back, core_matrix)


def settle_kernel(npart, ngrow, ngcol, npair, plan_ref, lad_ref, out_ref, row_ref, sum_ref, held_ref, send_sem, recv_sem, wide_send, wide_recv):
    x, g, c = lax.axis_index("pair"), lax.axis_index("grow"), lax.axis_index("gcol")
    count = npart * ngrow
    me = x * ngrow + g

    def seat(k):
        other = lax.rem(me + k, count)
        return other, lax.div(other, ngrow), lax.rem(other, ngrow)

    barrier = pltpu.get_barrier_semaphore()

    def greet(device):
        pl.semaphore_signal(barrier, inc=1, device_id=device, device_id_type=MESH)

    for k in range(1, ngcol):
        greet((x, g, lax.rem(c + k, ngcol)))
    for k in range(1, count):
        _, xo, go = seat(k)
        greet((xo, go, c))
    pl.semaphore_wait(barrier, ngcol - 1 + count - 1)

    def near(k, at):
        to = lax.rem(c + k, ngcol)
        return pltpu.make_async_remote_copy(
            src_ref=lad_ref.at[:, to], dst_ref=row_ref.at[at], send_sem=send_sem.at[k], recv_sem=recv_sem.at[at],
            device_id=(x, g, to), device_id_type=MESH)

    def wide(k, at):
        _, xo, go = seat(k)
        return pltpu.make_async_remote_copy(
            src_ref=sum_ref.at[go], dst_ref=held_ref.at[at], send_sem=wide_send.at[k], recv_sem=wide_recv.at[at],
            device_id=(xo, go, c), device_id_type=MESH)

    for k in range(1, ngcol):
        near(k, c).start()
    total = lad_ref[:, c]
    for k in range(1, ngcol):
        source = lax.rem(c + k, ngcol)
        near(k, source).wait_recv()
        total = total + row_ref[source]
    sum_ref[...] = total
    for k in range(1, count):
        wide(k, me).start()
    held_ref[me] = sum_ref[g]
    for k in range(1, count):
        wide(k, seat(k)[0]).wait_recv()
    slots = out_ref.shape[0]
    done = [jnp.zeros(out_ref.shape[1:], F32) for _ in range(slots)]
    for part in range(npart):
        summed = jnp.sum(held_ref[part * ngrow : (part + 1) * ngrow], axis=0)
        for p in range(npair):
            for s in range(slots):
                done[s] = jnp.where(plan_ref[s] == part * npair + p, summed[p], done[s])
    for s in range(slots):
        out_ref[s] = done[s]
    for k in range(1, ngcol):
        near(k, c).wait_send()
    for k in range(1, count):
        wide(k, me).wait_send()


def settle(lad, plan, mesh_shape):
    npart, ngrow, ngcol = mesh_shape
    count = npart * ngrow
    _, _, padded, lanes = lad.shape
    npair = plan.shape[0]
    return pl.pallas_call(
        functools.partial(settle_kernel, npart, ngrow, ngcol, npair),
        out_shape=jax.ShapeDtypeStruct((npair, lanes), F32),
        in_specs=[pl.BlockSpec(memory_space=pltpu.SMEM), pl.BlockSpec(memory_space=pltpu.VMEM)],
        out_specs=pl.BlockSpec(memory_space=pltpu.VMEM),
        scratch_shapes=[
            pltpu.VMEM((ngcol, ngrow, padded, lanes), F32),
            pltpu.VMEM((ngrow, padded, lanes), F32),
            pltpu.VMEM((count, padded, lanes), F32),
            pltpu.SemaphoreType.DMA((ngcol,)),
            pltpu.SemaphoreType.DMA((ngcol,)),
            pltpu.SemaphoreType.DMA((count,)),
            pltpu.SemaphoreType.DMA((count,)),
        ],
        compiler_params=pltpu.CompilerParams(collective_id=1, has_side_effects=True),
        name="settle",
    )(plan, lad)


def solution(mesh):
    shape = (mesh.shape["pair"], mesh.shape["grow"], mesh.shape["gcol"])

    def local(core_matrix, pair_panels, amplitudes, pair_widths, batch_plan):
        left, right, proj, back = static_part(pair_panels, amplitudes, pair_widths, core_matrix, shape[1], shape[2])
        lad = rest(left, right, proj, back, pair_widths, core_matrix, shape[1], shape[2])
        width = amplitudes.shape[1] ** 2 // (shape[1] * shape[2])
        return settle(lad, batch_plan, shape)[:, :width]

    in_specs = (
        P("grow", "gcol"),
        P("pair", None, ("grow", "gcol")),
        P("pair", None, None),
        P("pair"),
        P("pair"),
    )
    out_specs = P("pair", ("grow", "gcol"))
    return jax.shard_map(local, mesh=mesh, in_specs=in_specs, out_specs=out_specs, check_vma=False)
```

```python
import functools

import jax
import jax.numpy as jnp
from jax import lax
from jax.experimental import pallas as pl
from jax.experimental.pallas import tpu as pltpu
from jax.sharding import PartitionSpec as P

MESH = pl.DeviceIdType.MESH
TILE = 768
F32 = jnp.float32
BF16 = jnp.bfloat16
GROUP = 8
STATIC = 16


def units():
    found = []
    for high in range(STATIC // GROUP):
        for low in range(high + 1):
            for turn in range(GROUP // 2 + 1 if low == high else GROUP):
                found.append((high, low, turn, high != low or turn % (GROUP // 2) != 0))
    return found


def turned(block, turn):
    return block if turn % GROUP == 0 else pltpu.roll(block, turn % GROUP, 0)


def static_kernel(
        ngrow, ngcol, step, width_ref, panel_ref, table_ref, core_ref, left_ref, right_ref, proj_ref, back_ref, z_ref,
        y_ref, v_ref, mix_ref, amps_ref, widths, send_sem, recv_sem, tree_send, tree_recv, own_sem, z_sem, in_sem):
    x, g, c = lax.axis_index("pair"), lax.axis_index("grow"), lax.axis_index("gcol")
    npair, depth, piece = panel_ref.shape
    half = depth // 2
    cols = core_ref.shape[1]
    steps = cols // step
    per = len(units()) * GROUP
    bits = ngrow.bit_length() - 1
    root = lax.div(c * ngrow, ngcol)
    first = lax.rem(c * ngrow, ngcol)

    def bit(value, b):
        return lax.rem(lax.div(value, 1 << b), 2)

    def flip(b):
        return g + (1 << b) * (1 - 2 * bit(g, b))

    differ = [lax.rem(bit(g, b) + bit(root, b), 2) for b in range(bits)]
    before = [jnp.int32(0)]
    for b in range(bits):
        before.append(before[-1] + differ[b])
    is_root = before[bits] == 0

    def order(t):
        both = jnp.minimum(c, ngcol - 1 - c)
        near = lax.div(t + 1, 2)
        inner = c + near * (1 - 2 * lax.rem(t, 2))
        outer = jnp.where(c < ngcol - 1 - c, c + t - both, c - t + both)
        return jnp.where(t <= 2 * both, inner, outer)

    def core_copy(t):
        rows = pl.ds(pl.multiple_of(order(t) * piece, 128), piece)
        return pltpu.make_async_copy(core_ref.at[rows, :], z_ref.at[rows, :], z_sem.at[t])

    def span(at):
        return pl.ds(pl.multiple_of(at * piece, 128), piece)

    brought = [
        pltpu.make_async_copy(panel_ref, left_ref.at[:, :, span(c)], in_sem.at[0]),
        pltpu.make_async_copy(table_ref, amps_ref, in_sem.at[1]),
        pltpu.make_async_copy(width_ref, widths, in_sem.at[2]),
    ]
    for copy in brought:
        copy.start()
    for t in range(ngcol):
        core_copy(t).start()

    barrier = pltpu.get_barrier_semaphore()

    def greet(device):
        pl.semaphore_signal(barrier, inc=1, device_id=device, device_id_type=MESH)

    expected = jnp.int32(0)
    for far in (1, 2):
        for way in (0, 1):
            other = c + far * (1 - 2 * way)
            there = jnp.logical_and(other >= 0, other < ngcol)
            expected += jnp.where(there, 1, 0)

            @pl.when(there)
            def _(other=other):
                greet((x, g, other))

    for b in range(bits):
        expected += jnp.where(before[b] == 0, 1, 0)

        @pl.when(before[b] == 0)
        def _(b=b):
            greet((x, flip(b), c))

    def clear(i, carry):
        v_ref[pl.ds(pl.multiple_of(i * per, GROUP), per), :] = jnp.zeros((per, cols), F32)
        return carry

    lax.fori_loop(0, npair, clear, 0)
    for copy in brought:
        copy.wait()

    def build(at):
        def one(p, carry):
            rows = left_ref[p, 0:STATIC, span(at)].astype(F32)
            block = [rows[GROUP * k : GROUP * (k + 1)] for k in range(STATIC // GROUP)]
            made = [block[high] * turned(block[low], -turn) for high, low, turn, _ in units()]
            for k in range(0, len(made), 2):
                both = jnp.concatenate(made[k : k + 2], axis=0).astype(BF16)
                y_ref[pl.ds(pl.multiple_of(p * per + GROUP * k, 16), 16), :] = both
            return carry

        lax.fori_loop(0, npair, one, 0)

    build(c)

    whole = npair * depth
    pick_row = lax.broadcasted_iota(jnp.int32, (depth, whole), 0)
    pick_col = lax.broadcasted_iota(jnp.int32, (depth, whole), 1)
    pick = jnp.where(lax.rem(pick_col, depth) == pick_row, 1.0, 0.0).astype(BF16)
    row = lax.broadcasted_iota(jnp.int32, (whole, whole), 0)
    col = lax.broadcasted_iota(jnp.int32, (whole, whole), 1)
    width = jnp.zeros((whole, whole), jnp.int32)
    for p in range(npair):
        width = jnp.where(lax.div(row, depth) == p, widths[p], width)
    keep = jnp.logical_and(lax.div(row, depth) == lax.div(col, depth), jnp.logical_and(lax.rem(row, depth) < width, lax.rem(col, depth) < width))
    spread = jnp.dot(amps_ref[...].reshape(whole, depth), pick, preferred_element_type=F32)
    mix_ref[...] = jnp.where(keep, spread, 0.0).astype(BF16)

    pl.semaphore_wait(barrier, expected)

    def spot(ref, h, at):
        return ref.at[:, h * half : (h + 1) * half, span(at)]

    def hop(h, at, far, way, own):
        return pltpu.make_async_remote_copy(
            src_ref=panel_ref.at[:, h * half : (h + 1) * half, :] if own else spot(left_ref, h, at), dst_ref=spot(left_ref, h, at),
            send_sem=send_sem.at[h, at, far - 1, way], recv_sem=recv_sem.at[h, at],
            device_id=(x, g, c + far * (1 - 2 * way)), device_id_type=MESH)

    def branch(b, h, j, at):
        return pltpu.make_async_remote_copy(
            src_ref=spot(right_ref, h, j) if at is None else spot(left_ref, h, at), dst_ref=spot(right_ref, h, j),
            send_sem=tree_send.at[b, h, j], recv_sem=tree_recv.at[h, j],
            device_id=(x, flip(b), c), device_id_type=MESH)

    def own_right(h, j, at):
        return pltpu.make_async_copy(spot(left_ref, h, at), spot(right_ref, h, j), own_sem.at[h, j])

    def arrivals(s):
        return [(c - s, 0, c - s >= 0)] if s == 0 else [(c - s, 0, c - s >= 0), (c + s, 1, c + s <= ngcol - 1)]

    def inside(at):
        return jnp.logical_and(at >= first, at < first + ngrow)

    def onward(h, far, s, act):
        ways = [(c, 0, c >= 0), (c, 1, c >= 0)] if s == 0 else arrivals(s)
        for at, way, valid in ways:
            other = c + far * (1 - 2 * way)

            @pl.when(jnp.logical_and(valid, jnp.logical_and(other >= 0, other < ngcol)))
            def _(at=at, way=way):
                act(hop(h, at, far, way, s == 0))

    def start(copy):
        copy.start()

    def wait_send(copy):
        copy.wait_send()

    def to_tree(h, s):
        for at, _, valid in arrivals(s):
            @pl.when(jnp.logical_and(is_root, jnp.logical_and(valid, inside(at))))
            def _(at=at):
                for b in reversed(range(bits)):
                    branch(b, h, at - first, at).start()
                own_right(h, at - first, at).start()

    def take(h, s):
        for at, _, valid in arrivals(s):
            @pl.when(valid)
            def _(at=at):
                hop(h, at, 1, 0, False).wait_recv()

        if s % 2 == 0:
            onward(h, 1, s, start)
            if h == 1:
                onward(h, 2, s, start)
        to_tree(h, s)
        if h == 0 and s % 2 == 0:
            onward(h, 2, s, start)
        if h == 0 and s == 2:
            onward(1, 2, 0, start)

    def tree(h, s):
        for at, _, valid in arrivals(s):
            here = jnp.logical_and(valid, inside(at))

            @pl.when(jnp.logical_and(is_root, here))
            def _(at=at):
                own_right(h, at - first, at).wait()

            @pl.when(jnp.logical_and(jnp.logical_not(is_root), here))
            def _(at=at):
                branch(0, h, at - first, None).wait_recv()
                for b in range(bits):
                    @pl.when(before[b + 1] == 0)
                    def _(b=b):
                        branch(b, h, at - first, None).start()

    onward(0, 1, 0, start)
    onward(0, 2, 0, start)
    onward(1, 1, 0, start)
    to_tree(0, 0)
    to_tree(1, 0)

    plan = {}
    for t in range(1, ngcol - 1):
        plan.setdefault(t * steps, []).append((take, 0, t))
        plan.setdefault(t * steps + steps // 2, []).extend([(tree, 0, t - 1)] + ([(tree, 1, 0)] if t == 1 else [(take, 1, t - 1)]))

    def gain(i, t, s):
        wide = pl.ds(pl.multiple_of(s * step, 128), step)
        v_ref[:, wide] += jnp.dot(y_ref[...], z_ref[span(order(t)), wide], preferred_element_type=F32)

    def early(i, carry):
        t, s = lax.div(i, steps), lax.rem(i, steps)
        for when, jobs in plan.items():
            @pl.when(i == when)
            def _(jobs=jobs):
                for job, h, distance in jobs:
                    job(h, distance)

        for k in range(ngcol - 1):
            @pl.when(i == k * steps)
            def _(k=k):
                core_copy(k).wait()

        @pl.when(jnp.logical_and(s == 0, t > 0))
        def _():
            build(order(t))

        gain(i, t, s)
        return carry

    lax.fori_loop(0, (ngcol - 1) * steps, early, 0)

    take(0, ngcol - 1)
    last = ngcol - 1
    build(order(last))
    core_copy(last).wait()

    def fold(wide):
        def one(p, carry):
            proj = proj_ref[pl.ds(pl.multiple_of(p * depth, depth), STATIC), wide].astype(F32)
            block = [proj[GROUP * k : GROUP * (k + 1)] for k in range(STATIC // GROUP)]
            total = [None] * len(block)
            for k, (high, low, turn, both) in enumerate(units()):
                v = v_ref[pl.ds(pl.multiple_of(p * per, GROUP) + GROUP * k, GROUP), wide]
                straight = v * turned(block[low], -turn)
                total[high] = straight if total[high] is None else total[high] + straight
                if both:
                    cross = turned(v * block[high], turn)
                    total[low] = cross if total[low] is None else total[low] + cross
            for k, value in enumerate(total):
                back_ref[pl.ds(pl.multiple_of(p * STATIC, STATIC) + GROUP * k, GROUP), wide] = value
            return carry

        lax.fori_loop(0, npair, one, 0)

    def late(k):
        at = order(k)

        @pl.when(inside(at))
        def _():
            here = span(at - first)
            right = right_ref[:, :, here].reshape(whole, piece)
            proj_ref[:, here] = jnp.dot(mix_ref[...], right, preferred_element_type=F32).astype(BF16)

            def one(s, carry):
                wide = pl.ds(pl.multiple_of((at - first) * piece + s * step, 128), step)
                v_ref[:, wide] += jnp.dot(y_ref[...], z_ref[span(order(last)), wide], preferred_element_type=F32)
                fold(wide)
                return carry

            lax.fori_loop(0, piece // step, one, 0)

    for k in range(ngcol):
        if k == 0 and ngcol == 2:
            take(1, 1)
        if 1 <= k < ngcol - 1 and k + 1 >= ngcol - 2:
            take(1, k + 1)
        if k >= ngcol - 2:
            tree(0, k)
        if k >= 1:
            tree(1, k)
        late(k)

    for h in (0, 1):
        for s in range(0, ngcol, 2):
            onward(h, 1, s, wait_send)
            onward(h, 2, s, wait_send)
        for s in range(ngcol):
            for at, _, valid in arrivals(s):
                here = jnp.logical_and(valid, inside(at))
                for b in range(bits):
                    @pl.when(jnp.logical_and(before[b + 1] == 0, here))
                    def _(at=at, b=b):
                        branch(b, h, at - first, None).wait_send()


def static_part(panels, amplitudes, widths, core_matrix, ngrow, ngcol):
    npair, depth, piece = panels.shape
    rows, cols = core_matrix.shape
    step = 256 if piece % 256 == 0 else 128
    made = npair * len(units()) * GROUP
    bits = ngrow.bit_length() - 1
    vmem = pl.BlockSpec(memory_space=pltpu.VMEM)
    return pl.pallas_call(
        functools.partial(static_kernel, ngrow, ngcol, step),
        out_shape=(
            jax.ShapeDtypeStruct((npair, depth, rows), BF16),
            jax.ShapeDtypeStruct((npair, depth, cols), BF16),
            jax.ShapeDtypeStruct((npair * depth, cols), BF16),
            jax.ShapeDtypeStruct((npair * STATIC, cols), F32),
            jax.ShapeDtypeStruct((rows, cols), BF16),
        ),
        in_specs=[pl.BlockSpec(memory_space=pltpu.HBM)] * 4,
        out_specs=[vmem] * 5,
        scratch_shapes=[
            pltpu.VMEM((made, piece), BF16),
            pltpu.VMEM((made, cols), F32),
            pltpu.VMEM((npair * depth, npair * depth), BF16),
            pltpu.VMEM(amplitudes.shape, BF16),
            pltpu.SMEM(widths.shape, jnp.int32),
            pltpu.SemaphoreType.DMA((2, ngcol, 2, 2)),
            pltpu.SemaphoreType.DMA((2, ngcol)),
            pltpu.SemaphoreType.DMA((bits, 2, ngrow)),
            pltpu.SemaphoreType.DMA((2, ngrow)),
            pltpu.SemaphoreType.DMA((2, ngrow)),
            pltpu.SemaphoreType.DMA((ngcol,)),
            pltpu.SemaphoreType.DMA((3,)),
        ],
        compiler_params=pltpu.CompilerParams(collective_id=0, has_side_effects=True, vmem_limit_bytes=22 << 20),
        name="static_part",
    )(widths, panels, amplitudes, core_matrix)


def rest_kernel(widths, left_ref, right_ref, proj_ref, back_ref, z_ref, out_ref, y_ref, x_ref, v_ref, p_ref, g_ref, sum_ref, lad_ref):
    npair, depth, rows = left_ref.shape
    cols = z_ref.shape[1]
    tile = v_ref.shape[1]
    whole = npair * depth
    groups = depth // GROUP
    skip = STATIC // GROUP

    def duos(p):
        return lax.div(widths[p] + 1, 2)

    def rows_in(p):
        count = duos(p)
        found = jnp.int32(0)
        for group in range(skip, groups):
            found += 16 * (group + 1) * jnp.clip(count - 4 * group, 0, 4)
        return found

    def each_duo(p, offset, body):
        count = duos(p)
        for group in range(skip, groups):
            low = 4 * group
            begin = offset

            def run(duo, carry, group=group, low=low, begin=begin):
                body(group, 2 * duo, pl.multiple_of(begin + 16 * (group + 1) * (duo - low), 16))
                return carry

            lax.fori_loop(low, jnp.clip(count, low, low + 4), run, 0)
            offset = offset + 16 * (group + 1) * jnp.clip(count - low, 0, 4)

    def build(p, offset):
        x_ref[...] = left_ref[p].astype(F32)

        def duo(group, a, base):
            first, second = x_ref[pl.ds(a, 1), :], x_ref[pl.ds(a + 1, 1), :]
            for other in range(group + 1):
                block = x_ref[GROUP * other : GROUP * (other + 1), :]
                both = jnp.concatenate([first * block, second * block], axis=0)
                y_ref[pl.ds(base + 16 * other, 16), :] = both.astype(BF16)

        each_duo(p, offset, duo)
        return offset + rows_in(p)

    total = lax.fori_loop(0, npair, build, jnp.int32(0))
    sum_ref[...] = jnp.zeros_like(sum_ref)
    sizes = (512, 256, 128)

    for j in range(cols // tile):
        lanes = slice(j * tile, (j + 1) * tile)

        def multiply(size, base, i, carry):
            at = pl.ds(pl.multiple_of(base + i * size, 128), size)
            v_ref[at, :] = jnp.dot(y_ref[at, :], z_ref[:, lanes], preferred_element_type=F32)
            return carry

        done = jnp.int32(0)
        for size in sizes:
            count = lax.div(total - done + (0 if size > sizes[-1] else size - 1), size)
            lax.fori_loop(0, count, functools.partial(multiply, size, done), 0)
            done = done + count * size

        def fold(p, offset):
            mine = pl.ds(pl.multiple_of(p * depth, depth), depth)
            low = pl.ds(pl.multiple_of(p * depth, depth), STATIC)
            high = pl.ds(pl.multiple_of(p * depth, depth) + STATIC, depth - STATIC)
            p_ref[...] = proj_ref[mine, lanes].astype(F32)
            g_ref[low, :] = back_ref[pl.ds(pl.multiple_of(p * STATIC, STATIC), STATIC), lanes]
            g_ref[high, :] = jnp.zeros((depth - STATIC, tile), F32)
            origin = p * depth

            def duo(group, a, base):
                first, second = p_ref[pl.ds(a, 1), :], p_ref[pl.ds(a + 1, 1), :]
                sum0 = sum1 = None
                for other in range(group + 1):
                    upper = v_ref[pl.ds(base + 16 * other, 8), :]
                    lower = v_ref[pl.ds(base + 16 * other + 8, 8), :]
                    proj = p_ref[GROUP * other : GROUP * (other + 1), :]
                    sum0 = upper * proj if sum0 is None else sum0 + upper * proj
                    sum1 = lower * proj if sum1 is None else sum1 + lower * proj
                    if other < group:
                        g_ref[pl.ds(pl.multiple_of(origin, depth) + GROUP * other, GROUP), :] += upper * first + lower * second
                g_ref[pl.ds(origin + a, 1), :] += jnp.sum(sum0, axis=0, keepdims=True)
                g_ref[pl.ds(origin + a + 1, 1), :] += jnp.sum(sum1, axis=0, keepdims=True)

            each_duo(p, offset, duo)
            return offset + rows_in(p)

        lax.fori_loop(0, npair, fold, jnp.int32(0))
        sum_ref[...] += lax.dot_general(
            g_ref[...].astype(BF16), right_ref[:, :, lanes].reshape(whole, tile), (((1,), (1,)), ((), ())), preferred_element_type=F32)

    out_ref[...] = jnp.zeros_like(out_ref)
    ngrow, ngcol, padded, lanes = out_ref.shape
    share = depth // (ngrow * ngcol)
    for p in range(npair):
        width = widths[p]
        live = jnp.logical_and(
            lax.broadcasted_iota(jnp.int32, (depth, depth), 0) < width,
            lax.broadcasted_iota(jnp.int32, (depth, depth), 1) < width)
        lad_ref[...] = jnp.where(live, sum_ref[depth * p : depth * (p + 1), depth * p : depth * (p + 1)], 0.0)
        parts = [lad_ref[pl.ds(r, ngrow * ngcol, stride=share), :] for r in range(share)]
        row = parts[0] if share == 1 else jnp.concatenate(parts, axis=1)
        for at in range(ngrow):
            out_ref[at, :, p, 0 : share * depth] = row[at * ngcol : (at + 1) * ngcol]


def rest(left, right, proj, back, core, widths, ngrow, ngcol):
    npair, depth, rows = left.shape
    cols = core.shape[1]
    tile = TILE if cols % TILE == 0 else cols // 2
    most = npair * sum(16 * (group + 1) * 4 for group in range(STATIC // GROUP, depth // GROUP))
    most = -(-most // 128) * 128
    padded = -(-npair // 8) * 8
    vmem = pl.BlockSpec(memory_space=pltpu.VMEM)
    return pl.pallas_call(
        rest_kernel,
        out_shape=jax.ShapeDtypeStruct((ngrow, ngcol, padded, 128), F32),
        in_specs=[pl.BlockSpec(memory_space=pltpu.SMEM)] + [vmem] * 5,
        out_specs=vmem,
        scratch_shapes=[
            pltpu.VMEM((most, rows), BF16),
            pltpu.VMEM((depth, rows), F32),
            pltpu.VMEM((most, tile), F32),
            pltpu.VMEM((depth, tile), F32),
            pltpu.VMEM((npair * depth, tile), F32),
            pltpu.VMEM((npair * depth, npair * depth), F32),
            pltpu.VMEM((depth, depth), F32),
        ],
        compiler_params=pltpu.CompilerParams(vmem_limit_bytes=30 << 20),
        name="rest",
    )(widths, left, right, proj, back, core)


def settle_kernel(npart, ngrow, ngcol, npair, plan_ref, lad_ref, out_ref, row_ref, sum_ref, held_ref, send_sem, recv_sem, wide_send, wide_recv):
    x, g, c = lax.axis_index("pair"), lax.axis_index("grow"), lax.axis_index("gcol")
    count = npart * ngrow
    me = x * ngrow + g

    def seat(k):
        other = lax.rem(me + k, count)
        return other, lax.div(other, ngrow), lax.rem(other, ngrow)

    barrier = pltpu.get_barrier_semaphore()

    def greet(device):
        pl.semaphore_signal(barrier, inc=1, device_id=device, device_id_type=MESH)

    for k in range(1, ngcol):
        greet((x, g, lax.rem(c + k, ngcol)))
    for k in range(1, count):
        _, xo, go = seat(k)
        greet((xo, go, c))
    pl.semaphore_wait(barrier, ngcol - 1 + count - 1)

    def near(k, at):
        to = lax.rem(c + k, ngcol)
        return pltpu.make_async_remote_copy(
            src_ref=lad_ref.at[:, to], dst_ref=row_ref.at[at], send_sem=send_sem.at[k], recv_sem=recv_sem.at[at],
            device_id=(x, g, to), device_id_type=MESH)

    def wide(k, at):
        _, xo, go = seat(k)
        return pltpu.make_async_remote_copy(
            src_ref=sum_ref.at[go], dst_ref=held_ref.at[at], send_sem=wide_send.at[k], recv_sem=wide_recv.at[at],
            device_id=(xo, go, c), device_id_type=MESH)

    for k in range(1, ngcol):
        near(k, c).start()
    total = lad_ref[:, c]
    for k in range(1, ngcol):
        source = lax.rem(c + k, ngcol)
        near(k, source).wait_recv()
        total = total + row_ref[source]
    sum_ref[...] = total
    for k in range(1, count):
        wide(k, me).start()
    held_ref[me] = sum_ref[g]
    for k in range(1, count):
        wide(k, seat(k)[0]).wait_recv()
    slots = out_ref.shape[0]
    done = [jnp.zeros(out_ref.shape[1:], F32) for _ in range(slots)]
    for part in range(npart):
        summed = jnp.sum(held_ref[part * ngrow : (part + 1) * ngrow], axis=0)
        for p in range(npair):
            for s in range(slots):
                done[s] = jnp.where(plan_ref[s] == part * npair + p, summed[p], done[s])
    for s in range(slots):
        out_ref[s] = done[s]
    for k in range(1, ngcol):
        near(k, c).wait_send()
    for k in range(1, count):
        wide(k, me).wait_send()


def settle(lad, plan, mesh_shape):
    npart, ngrow, ngcol = mesh_shape
    count = npart * ngrow
    _, _, padded, lanes = lad.shape
    npair = plan.shape[0]
    return pl.pallas_call(
        functools.partial(settle_kernel, npart, ngrow, ngcol, npair),
        out_shape=jax.ShapeDtypeStruct((npair, lanes), F32),
        in_specs=[pl.BlockSpec(memory_space=pltpu.SMEM), pl.BlockSpec(memory_space=pltpu.VMEM)],
        out_specs=pl.BlockSpec(memory_space=pltpu.VMEM),
        scratch_shapes=[
            pltpu.VMEM((ngcol, ngrow, padded, lanes), F32),
            pltpu.VMEM((ngrow, padded, lanes), F32),
            pltpu.VMEM((count, padded, lanes), F32),
            pltpu.SemaphoreType.DMA((ngcol,)),
            pltpu.SemaphoreType.DMA((ngcol,)),
            pltpu.SemaphoreType.DMA((count,)),
            pltpu.SemaphoreType.DMA((count,)),
        ],
        compiler_params=pltpu.CompilerParams(collective_id=1, has_side_effects=True, vmem_limit_bytes=8 << 20),
        name="settle",
    )(plan, lad)


def solution(mesh):
    shape = (mesh.shape["pair"], mesh.shape["grow"], mesh.shape["gcol"])

    def local(core_matrix, pair_panels, amplitudes, pair_widths, batch_plan):
        pinned = [pltpu.with_memory_space_constraint(array, pltpu.HBM) for array in (pair_panels, amplitudes, pair_widths, core_matrix)]
        left, right, proj, back, core = static_part(*pinned, shape[1], shape[2])
        lad = rest(left, right, proj, back, core, pair_widths, shape[1], shape[2])
        width = amplitudes.shape[1] ** 2 // (shape[1] * shape[2])
        return settle(lad, batch_plan, shape)[:, :width]

    in_specs = (
        P("grow", "gcol"),
        P("pair", None, ("grow", "gcol")),
        P("pair", None, None),
        P("pair"),
        P("pair"),
    )
    out_specs = P("pair", ("grow", "gcol"))
    return jax.shard_map(local, mesh=mesh, in_specs=in_specs, out_specs=out_specs, check_vma=False)
```

```python
import functools

import jax
import jax.numpy as jnp
from jax import lax
from jax.experimental import pallas as pl
from jax.experimental.pallas import tpu as pltpu
from jax.sharding import PartitionSpec as P

MESH = pl.DeviceIdType.MESH
TILE = 768
F32 = jnp.float32
BF16 = jnp.bfloat16
GROUP = 8
STATIC = 16


def units():
    found = []
    for high in range(STATIC // GROUP):
        for low in range(high + 1):
            for turn in range(GROUP // 2 + 1 if low == high else GROUP):
                found.append((high, low, turn, high != low or turn % (GROUP // 2) != 0))
    return found


def turned(block, turn):
    return block if turn % GROUP == 0 else pltpu.roll(block, turn % GROUP, 0)


def static_kernel(
        ngrow, ngcol, step, width_ref, panel_ref, table_ref, core_ref, left_ref, right_ref, proj_ref, back_ref, z_ref,
        y_ref, v_ref, mix_ref, amps_ref, widths, send_sem, high_sem, recv_sem, tree_send, tree_recv, own_sem, z_sem, in_sem):
    x, g, c = lax.axis_index("pair"), lax.axis_index("grow"), lax.axis_index("gcol")
    npair, depth, piece = panel_ref.shape
    half = depth // 2
    whole = npair * depth
    cols = core_ref.shape[1]
    steps = cols // step
    per = len(units()) * GROUP
    bits = ngrow.bit_length() - 1
    root = lax.div(c * ngrow, ngcol)
    first = lax.rem(c * ngrow, ngcol)

    def bit(value, b):
        return lax.rem(lax.div(value, 1 << b), 2)

    def flip(b):
        return g + (1 << b) * (1 - 2 * bit(g, b))

    differ = [lax.rem(bit(g, b) + bit(root, b), 2) for b in range(bits)]
    before = [jnp.int32(0)]
    for b in range(bits):
        before.append(before[-1] + differ[b])
    is_root = before[bits] == 0

    toward = lax.div(g * ngcol + ngrow - 1, ngrow)
    until = lax.div((g + 1) * ngcol - 1, ngrow)

    def order(t):
        both = jnp.minimum(c, ngcol - 1 - c)
        near = lax.div(t + 1, 2)
        inner = c + near * (1 - 2 * lax.rem(t, 2))
        outer = jnp.where(c < ngcol - 1 - c, c + t - both, c - t + both)
        return jnp.where(t <= 2 * both, inner, outer)

    def core_copy(t):
        rows = pl.ds(pl.multiple_of(order(t) * piece, 128), piece)
        return pltpu.make_async_copy(core_ref.at[rows, :], z_ref.at[rows, :], z_sem.at[t])

    def span(at):
        return pl.ds(pl.multiple_of(at * piece, 128), piece)

    brought = [
        pltpu.make_async_copy(panel_ref, left_ref.at[:, :, span(c)], in_sem.at[0]),
        pltpu.make_async_copy(table_ref, amps_ref, in_sem.at[1]),
        pltpu.make_async_copy(width_ref, widths, in_sem.at[2]),
    ]
    for copy in brought:
        copy.start()
    core_copy(0).start()

    barrier = pltpu.get_barrier_semaphore()

    def greet(device):
        pl.semaphore_signal(barrier, inc=1, device_id=device, device_id_type=MESH)

    expected = jnp.int32(0)
    for far in range(1, ngcol):
        for way in (0, 1):
            other = c + far * (1 - 2 * way)
            there = jnp.logical_and(other >= 0, other < ngcol)
            expected += jnp.where(there, 1, 0)

            @pl.when(there)
            def _(other=other):
                greet((x, g, other))

    for b in range(bits):
        expected += jnp.where(before[b] == 0, 1, 0)

        @pl.when(before[b] == 0)
        def _(b=b):
            greet((x, flip(b), c))

    def clear(i, carry):
        v_ref[pl.ds(pl.multiple_of(i * per, GROUP), per), :] = jnp.zeros((per, cols), F32)
        return carry

    lax.fori_loop(0, npair, clear, 0)
    def build(at):
        def one(p, carry):
            rows = left_ref[p, 0:STATIC, span(at)].astype(F32)
            block = [rows[GROUP * k : GROUP * (k + 1)] for k in range(STATIC // GROUP)]
            made = [block[high] * turned(block[low], -turn) for high, low, turn, _ in units()]
            for k in range(0, len(made), 2):
                both = jnp.concatenate(made[k : k + 2], axis=0).astype(BF16)
                y_ref[pl.ds(pl.multiple_of(p * per + GROUP * k, 16), 16), :] = both
            return carry

        lax.fori_loop(0, npair, one, 0)

    pl.semaphore_wait(barrier, expected)

    def spot(ref, h, at):
        return ref.at[:, h * half : (h + 1) * half, span(at)]

    def hop(h, at, far, way, own):
        return pltpu.make_async_remote_copy(
            src_ref=panel_ref.at[:, h * half : (h + 1) * half, :] if own else spot(left_ref, h, at), dst_ref=spot(left_ref, h, at),
            send_sem=send_sem.at[at, far - 1, way] if h == 0 else high_sem.at[far - 1, way], recv_sem=recv_sem.at[h, at],
            device_id=(x, g, c + far * (1 - 2 * way)), device_id_type=MESH)

    def branch(b, h, j, at):
        return pltpu.make_async_remote_copy(
            src_ref=spot(right_ref, h, j) if at is None else spot(left_ref, h, at), dst_ref=spot(right_ref, h, j),
            send_sem=tree_send.at[b, h, j], recv_sem=tree_recv.at[h, j],
            device_id=(x, flip(b), c), device_id_type=MESH)

    def own_right(h, j, at):
        return pltpu.make_async_copy(spot(left_ref, h, at), spot(right_ref, h, j), own_sem.at[h, j])

    def arrivals(s):
        return [(c - s, 0, c - s >= 0)] if s == 0 else [(c - s, 0, c - s >= 0), (c + s, 1, c + s <= ngcol - 1)]

    def inside(at):
        return jnp.logical_and(at >= first, at < first + ngrow)

    def onward(far, s, act):
        ways = [(c, 0, c >= 0), (c, 1, c >= 0)] if s == 0 else arrivals(s)
        for at, way, valid in ways:
            other = c + far * (1 - 2 * way)

            @pl.when(jnp.logical_and(valid, jnp.logical_and(other >= 0, other < ngcol)))
            def _(at=at, way=way):
                act(hop(0, at, far, way, s == 0))

    def upward(stage, act):
        for far in range(1, ngcol):
            for way in (0, 1):
                other = c + far * (1 - 2 * way)
                there = jnp.logical_and(other >= 0, other < ngcol)
                rooted = jnp.logical_and(other >= toward, other <= until)
                free = (c < 2 if way == 0 else c > ngcol - 3) if far == 1 else c < 0
                chosen = (rooted, jnp.logical_and(jnp.logical_not(rooted), free), jnp.logical_not(jnp.logical_or(rooted, free)), c >= 0)[stage]

                @pl.when(jnp.logical_and(there, chosen))
                def _(far=far, way=way):
                    act(hop(1, c, far, way, True))

    def start(copy):
        copy.start()

    def wait_send(copy):
        copy.wait_send()

    def to_tree(h, s):
        for at, _, valid in arrivals(s):
            @pl.when(jnp.logical_and(is_root, jnp.logical_and(valid, inside(at))))
            def _(at=at):
                for b in reversed(range(bits)):
                    branch(b, h, at - first, at).start()
                own_right(h, at - first, at).start()

    def lower(s):
        for at, _, valid in arrivals(s):
            @pl.when(valid)
            def _(at=at):
                hop(0, at, 1, 0, False).wait_recv()

        if s % 2 == 0:
            onward(1, s, start)
            onward(2, s, start)
        to_tree(0, s)
        if s == min(2, ngcol - 1):
            upward(2, start)

    def take_upper(s, root):
        for at, _, valid in arrivals(s):
            @pl.when(jnp.logical_and(valid, is_root if root else jnp.logical_not(is_root)))
            def _(at=at):
                hop(1, at, 1, 0, False).wait_recv()

    def upper(s):
        take_upper(s, True)
        to_tree(1, s)

    def tree(h, s):
        for at, _, valid in arrivals(s):
            here = jnp.logical_and(valid, inside(at))

            @pl.when(jnp.logical_and(is_root, here))
            def _(at=at):
                own_right(h, at - first, at).wait()

            @pl.when(jnp.logical_and(jnp.logical_not(is_root), here))
            def _(at=at):
                branch(0, h, at - first, None).wait_recv()
                for b in range(bits):
                    @pl.when(before[b + 1] == 0)
                    def _(b=b):
                        branch(b, h, at - first, None).start()

    onward(1, 0, start)
    onward(2, 0, start)
    upward(0, start)
    upward(1, start)

    for copy in brought:
        copy.wait()

    to_tree(0, 0)
    to_tree(1, 0)

    build(c)

    pick_row = lax.broadcasted_iota(jnp.int32, (depth, whole), 0)
    pick_col = lax.broadcasted_iota(jnp.int32, (depth, whole), 1)
    pick = jnp.where(lax.rem(pick_col, depth) == pick_row, 1.0, 0.0).astype(BF16)
    row = lax.broadcasted_iota(jnp.int32, (whole, whole), 0)
    col = lax.broadcasted_iota(jnp.int32, (whole, whole), 1)
    width = jnp.zeros((whole, whole), jnp.int32)
    for p in range(npair):
        width = jnp.where(lax.div(row, depth) == p, widths[p], width)
    keep = jnp.logical_and(lax.div(row, depth) == lax.div(col, depth), jnp.logical_and(lax.rem(row, depth) < width, lax.rem(col, depth) < width))
    spread = jnp.dot(amps_ref[...].reshape(whole, depth), pick, preferred_element_type=F32)
    mix_ref[...] = jnp.where(keep, spread, 0.0).astype(BF16)

    def low_tree(s):
        tree(0, s)

    def high_tree(s):
        tree(1, s)

    plan = {}
    end = (ngcol - 1) * steps

    def at_step(position, job, distance):
        plan.setdefault(position, []).append((job, distance))

    for t in range(1, ngcol):
        at_step(t * steps - (t > 1), lower, t)
    at_step(end - steps, low_tree, 0)
    at_step(end - steps, high_tree, 0)
    for t in range(1, ngcol):
        at_step(end + (t - 3 if t > 2 else 2 * t - 5), upper, t)
    for t in range(1, ngcol):
        at_step(end + (t if t > 1 else 0), high_tree, t)
        at_step(end + (t - 1 if t > 1 else -2), low_tree, t)

    def gain(i, t, s):
        wide = pl.ds(pl.multiple_of(s * step, 128), step)
        v_ref[:, wide] += jnp.dot(y_ref[...], z_ref[span(order(t)), wide], preferred_element_type=F32)

    def early(i, carry):
        t, s = lax.div(i, steps), lax.rem(i, steps)
        for when, jobs in plan.items():
            if when >= end:
                continue

            @pl.when(i == when)
            def _(jobs=jobs):
                for job, distance in jobs:
                    job(distance)

        for k in range(ngcol - 1):
            @pl.when(i == k * steps)
            def _(k=k):
                core_copy(k).wait()
                core_copy(k + 1).start()

        @pl.when(jnp.logical_and(s == 0, t > 0))
        def _():
            build(order(t))

        gain(i, t, s)
        return carry

    lax.fori_loop(0, (ngcol - 1) * steps, early, 0)

    last = ngcol - 1
    build(order(last))
    core_copy(last).wait()

    def fold(wide):
        def one(p, carry):
            proj = proj_ref[pl.ds(pl.multiple_of(p * depth, depth), STATIC), wide].astype(F32)
            block = [proj[GROUP * k : GROUP * (k + 1)] for k in range(STATIC // GROUP)]
            total = [None] * len(block)
            for k, (high, low, turn, both) in enumerate(units()):
                v = v_ref[pl.ds(pl.multiple_of(p * per, GROUP) + GROUP * k, GROUP), wide]
                straight = v * turned(block[low], -turn)
                total[high] = straight if total[high] is None else total[high] + straight
                if both:
                    cross = turned(v * block[high], turn)
                    total[low] = cross if total[low] is None else total[low] + cross
            for k, value in enumerate(total):
                back_ref[pl.ds(pl.multiple_of(p * STATIC, STATIC) + GROUP * k, GROUP), wide] = value
            return carry

        lax.fori_loop(0, npair, one, 0)

    fine = 256 if piece % 256 == 0 else 128

    def late(k, carry):
        at = order(k)
        for when, jobs in plan.items():
            if when < end:
                continue

            @pl.when(k == when - end)
            def _(jobs=jobs):
                for job, distance in jobs:
                    job(distance)

        @pl.when(inside(at))
        def _():
            here = span(at - first)
            right = right_ref[:, :, here].reshape(whole, piece)
            proj_ref[:, here] = jnp.dot(mix_ref[...], right, preferred_element_type=F32).astype(BF16)
            v_ref[:, here] += jnp.dot(y_ref[...], z_ref[span(order(last)), here], preferred_element_type=F32)

            def part(n, carry):
                fold(pl.ds(pl.multiple_of((at - first) * piece + n * fine, 128), fine))
                return carry

            lax.fori_loop(0, piece // fine, part, 0)

        return carry

    lax.fori_loop(0, ngcol, late, 0)
    for s in range(1, ngcol):
        take_upper(s, False)

    upward(3, wait_send)
    for s in range(0, ngcol, 2):
        onward(1, s, wait_send)
        onward(2, s, wait_send)
    for s in range(ngcol):
        for at, _, valid in arrivals(s):
            here = jnp.logical_and(valid, inside(at))
            for h in (0, 1):
                for b in range(bits):
                    @pl.when(jnp.logical_and(before[b + 1] == 0, here))
                    def _(at=at, b=b, h=h):
                        branch(b, h, at - first, None).wait_send()


def static_part(panels, amplitudes, widths, core_matrix, ngrow, ngcol):
    npair, depth, piece = panels.shape
    rows, cols = core_matrix.shape
    step = TILE if cols % TILE == 0 else piece
    made = npair * len(units()) * GROUP
    bits = ngrow.bit_length() - 1
    vmem = pl.BlockSpec(memory_space=pltpu.VMEM)
    return pl.pallas_call(
        functools.partial(static_kernel, ngrow, ngcol, step),
        out_shape=(
            jax.ShapeDtypeStruct((npair, depth, rows), BF16),
            jax.ShapeDtypeStruct((npair, depth, cols), BF16),
            jax.ShapeDtypeStruct((npair * depth, cols), BF16),
            jax.ShapeDtypeStruct((npair * STATIC, cols), F32),
            jax.ShapeDtypeStruct((rows, cols), BF16),
        ),
        in_specs=[pl.BlockSpec(memory_space=pltpu.HBM)] * 4,
        out_specs=[vmem] * 5,
        scratch_shapes=[
            pltpu.VMEM((made, piece), BF16),
            pltpu.VMEM((made, cols), F32),
            pltpu.VMEM((npair * depth, npair * depth), BF16),
            pltpu.VMEM(amplitudes.shape, BF16),
            pltpu.SMEM(widths.shape, jnp.int32),
            pltpu.SemaphoreType.DMA((ngcol, 2, 2)),
            pltpu.SemaphoreType.DMA((ngcol - 1, 2)),
            pltpu.SemaphoreType.DMA((2, ngcol)),
            pltpu.SemaphoreType.DMA((bits, 2, ngrow)),
            pltpu.SemaphoreType.DMA((2, ngrow)),
            pltpu.SemaphoreType.DMA((2, ngrow)),
            pltpu.SemaphoreType.DMA((ngcol,)),
            pltpu.SemaphoreType.DMA((3,)),
        ],
        compiler_params=pltpu.CompilerParams(collective_id=0, has_side_effects=True, vmem_limit_bytes=22 << 20),
        name="static_part",
    )(widths, panels, amplitudes, core_matrix)


def rest_kernel(widths, left_ref, right_ref, proj_ref, back_ref, z_ref, out_ref, y_ref, x_ref, v_ref, p_ref, g_ref, sum_ref, lad_ref):
    npair, depth, rows = left_ref.shape
    cols = z_ref.shape[1]
    tile = v_ref.shape[1]
    whole = npair * depth
    groups = depth // GROUP
    skip = STATIC // GROUP

    def duos(p):
        return lax.div(widths[p] + 1, 2)

    def rows_in(p):
        count = duos(p)
        found = jnp.int32(0)
        for group in range(skip, groups):
            found += 16 * (group + 1) * jnp.clip(count - 4 * group, 0, 4)
        return found

    def each_duo(p, offset, body):
        count = duos(p)
        for group in range(skip, groups):
            low = 4 * group
            begin = offset

            def run(duo, carry, group=group, low=low, begin=begin):
                body(group, 2 * duo, pl.multiple_of(begin + 16 * (group + 1) * (duo - low), 16))
                return carry

            lax.fori_loop(low, jnp.clip(count, low, low + 4), run, 0)
            offset = offset + 16 * (group + 1) * jnp.clip(count - low, 0, 4)

    def build(p, offset):
        x_ref[...] = left_ref[p].astype(F32)

        def duo(group, a, base):
            first, second = x_ref[pl.ds(a, 1), :], x_ref[pl.ds(a + 1, 1), :]
            for other in range(group + 1):
                block = x_ref[GROUP * other : GROUP * (other + 1), :]
                both = jnp.concatenate([first * block, second * block], axis=0)
                y_ref[pl.ds(base + 16 * other, 16), :] = both.astype(BF16)

        each_duo(p, offset, duo)
        return offset + rows_in(p)

    total = lax.fori_loop(0, npair, build, jnp.int32(0))
    sum_ref[...] = jnp.zeros_like(sum_ref)
    size, grain = 512, 128
    full = jnp.where(total > 0, lax.div(jnp.maximum(total - size // 2 - 1, 0), size), 0)
    left_over = total - full * size

    def column(j, carry):
        lanes = pl.ds(pl.multiple_of(j * tile, 128), tile)

        def multiply(base, count):
            at = pl.ds(base if isinstance(base, int) else pl.multiple_of(base, grain), count)
            v_ref[at, :] = jnp.dot(y_ref[at, :], z_ref[:, lanes], preferred_element_type=F32)

        def block(i, carry):
            multiply(i * size, size)
            return carry

        lax.fori_loop(0, full, block, 0)
        for count in range(grain, size + size // 2 + 1, grain):
            @pl.when(jnp.logical_and(left_over > count - grain, left_over <= count))
            def _(count=count):
                multiply(full * size, count)

        def fold(p, offset):
            mine = pl.ds(pl.multiple_of(p * depth, depth), depth)
            low = pl.ds(pl.multiple_of(p * depth, depth), STATIC)
            high = pl.ds(pl.multiple_of(p * depth, depth) + STATIC, depth - STATIC)
            p_ref[...] = proj_ref[mine, lanes].astype(F32)
            g_ref[low, :] = back_ref[pl.ds(pl.multiple_of(p * STATIC, STATIC), STATIC), lanes]
            g_ref[high, :] = jnp.zeros((depth - STATIC, tile), F32)
            origin = p * depth

            def duo(group, a, base):
                first, second = p_ref[pl.ds(a, 1), :], p_ref[pl.ds(a + 1, 1), :]
                sum0 = sum1 = None
                for other in range(group + 1):
                    upper = v_ref[pl.ds(base + 16 * other, 8), :]
                    lower = v_ref[pl.ds(base + 16 * other + 8, 8), :]
                    proj = p_ref[GROUP * other : GROUP * (other + 1), :]
                    sum0 = upper * proj if sum0 is None else sum0 + upper * proj
                    sum1 = lower * proj if sum1 is None else sum1 + lower * proj
                    if other < group:
                        g_ref[pl.ds(pl.multiple_of(origin, depth) + GROUP * other, GROUP), :] += upper * first + lower * second
                g_ref[pl.ds(origin + a, 1), :] += jnp.sum(sum0, axis=0, keepdims=True)
                g_ref[pl.ds(origin + a + 1, 1), :] += jnp.sum(sum1, axis=0, keepdims=True)

            each_duo(p, offset, duo)
            return offset + rows_in(p)

        lax.fori_loop(0, npair, fold, jnp.int32(0))
        sum_ref[...] += lax.dot_general(
            g_ref[...].astype(BF16), right_ref[:, :, lanes].reshape(whole, tile), (((1,), (1,)), ((), ())), preferred_element_type=F32)
        return carry

    lax.fori_loop(0, cols // tile, column, 0)

    out_ref[...] = jnp.zeros_like(out_ref)
    ngrow, ngcol, padded, lanes = out_ref.shape
    share = depth // (ngrow * ngcol)
    for p in range(npair):
        width = widths[p]
        live = jnp.logical_and(
            lax.broadcasted_iota(jnp.int32, (depth, depth), 0) < width,
            lax.broadcasted_iota(jnp.int32, (depth, depth), 1) < width)
        lad_ref[...] = jnp.where(live, sum_ref[depth * p : depth * (p + 1), depth * p : depth * (p + 1)], 0.0)
        parts = [lad_ref[pl.ds(r, ngrow * ngcol, stride=share), :] for r in range(share)]
        row = parts[0] if share == 1 else jnp.concatenate(parts, axis=1)
        for at in range(ngrow):
            out_ref[at, :, p, 0 : share * depth] = row[at * ngcol : (at + 1) * ngcol]


def rest(left, right, proj, back, core, widths, ngrow, ngcol):
    npair, depth, rows = left.shape
    cols = core.shape[1]
    tile = TILE if cols % TILE == 0 else cols // 2
    most = npair * sum(16 * (group + 1) * 4 for group in range(STATIC // GROUP, depth // GROUP))
    most = -(-most // 128) * 128
    padded = -(-npair // 8) * 8
    vmem = pl.BlockSpec(memory_space=pltpu.VMEM)
    return pl.pallas_call(
        rest_kernel,
        out_shape=jax.ShapeDtypeStruct((ngrow, ngcol, padded, 128), F32),
        in_specs=[pl.BlockSpec(memory_space=pltpu.SMEM)] + [vmem] * 5,
        out_specs=vmem,
        scratch_shapes=[
            pltpu.VMEM((most, rows), BF16),
            pltpu.VMEM((depth, rows), F32),
            pltpu.VMEM((most, tile), F32),
            pltpu.VMEM((depth, tile), F32),
            pltpu.VMEM((npair * depth, tile), F32),
            pltpu.VMEM((npair * depth, npair * depth), F32),
            pltpu.VMEM((depth, depth), F32),
        ],
        compiler_params=pltpu.CompilerParams(vmem_limit_bytes=30 << 20),
        name="rest",
    )(widths, left, right, proj, back, core)


def settle_kernel(npart, ngrow, ngcol, npair, plan_ref, lad_ref, out_ref, row_ref, sum_ref, held_ref, send_sem, recv_sem, wide_send, wide_recv):
    x, g, c = lax.axis_index("pair"), lax.axis_index("grow"), lax.axis_index("gcol")
    count = npart * ngrow
    me = x * ngrow + g

    def seat(k):
        other = lax.rem(me + k, count)
        return other, lax.div(other, ngrow), lax.rem(other, ngrow)

    barrier = pltpu.get_barrier_semaphore()

    def greet(device):
        pl.semaphore_signal(barrier, inc=1, device_id=device, device_id_type=MESH)

    for k in range(1, ngcol):
        greet((x, g, lax.rem(c + k, ngcol)))
    for k in range(1, count):
        _, xo, go = seat(k)
        greet((xo, go, c))
    pl.semaphore_wait(barrier, ngcol - 1 + count - 1)

    def near(k, at):
        to = lax.rem(c + k, ngcol)
        return pltpu.make_async_remote_copy(
            src_ref=lad_ref.at[:, to], dst_ref=row_ref.at[at], send_sem=send_sem.at[k], recv_sem=recv_sem.at[at],
            device_id=(x, g, to), device_id_type=MESH)

    def wide(k, at):
        _, xo, go = seat(k)
        return pltpu.make_async_remote_copy(
            src_ref=sum_ref.at[go], dst_ref=held_ref.at[at], send_sem=wide_send.at[k], recv_sem=wide_recv.at[at],
            device_id=(xo, go, c), device_id_type=MESH)

    for k in range(1, ngcol):
        near(k, c).start()
    total = lad_ref[:, c]
    for k in range(1, ngcol):
        source = lax.rem(c + k, ngcol)
        near(k, source).wait_recv()
        total = total + row_ref[source]
    sum_ref[...] = total
    for k in range(1, count):
        wide(k, me).start()
    held_ref[me] = sum_ref[g]
    for k in range(1, count):
        wide(k, seat(k)[0]).wait_recv()
    slots = out_ref.shape[0]
    done = [jnp.zeros(out_ref.shape[1:], F32) for _ in range(slots)]
    for part in range(npart):
        summed = jnp.sum(held_ref[part * ngrow : (part + 1) * ngrow], axis=0)
        for p in range(npair):
            for s in range(slots):
                done[s] = jnp.where(plan_ref[s] == part * npair + p, summed[p], done[s])
    for s in range(slots):
        out_ref[s] = done[s]
    for k in range(1, ngcol):
        near(k, c).wait_send()
    for k in range(1, count):
        wide(k, me).wait_send()


def settle(lad, plan, mesh_shape):
    npart, ngrow, ngcol = mesh_shape
    count = npart * ngrow
    _, _, padded, lanes = lad.shape
    npair = plan.shape[0]
    return pl.pallas_call(
        functools.partial(settle_kernel, npart, ngrow, ngcol, npair),
        out_shape=jax.ShapeDtypeStruct((npair, lanes), F32),
        in_specs=[pl.BlockSpec(memory_space=pltpu.SMEM), pl.BlockSpec(memory_space=pltpu.VMEM)],
        out_specs=pl.BlockSpec(memory_space=pltpu.VMEM),
        scratch_shapes=[
            pltpu.VMEM((ngcol, ngrow, padded, lanes), F32),
            pltpu.VMEM((ngrow, padded, lanes), F32),
            pltpu.VMEM((count, padded, lanes), F32),
            pltpu.SemaphoreType.DMA((ngcol,)),
            pltpu.SemaphoreType.DMA((ngcol,)),
            pltpu.SemaphoreType.DMA((count,)),
            pltpu.SemaphoreType.DMA((count,)),
        ],
        compiler_params=pltpu.CompilerParams(collective_id=1, has_side_effects=True, vmem_limit_bytes=8 << 20),
        name="settle",
    )(plan, lad)


def solution(mesh):
    shape = (mesh.shape["pair"], mesh.shape["grow"], mesh.shape["gcol"])

    def local(core_matrix, pair_panels, amplitudes, pair_widths, batch_plan):
        pinned = [pltpu.with_memory_space_constraint(array, pltpu.HBM) for array in (pair_panels, amplitudes, pair_widths, core_matrix)]
        left, right, proj, back, core = static_part(*pinned, shape[1], shape[2])
        lad = rest(left, right, proj, back, core, pair_widths, shape[1], shape[2])
        width = amplitudes.shape[1] ** 2 // (shape[1] * shape[2])
        return settle(lad, batch_plan, shape)[:, :width]

    in_specs = (
        P("grow", "gcol"),
        P("pair", None, ("grow", "gcol")),
        P("pair", None, None),
        P("pair"),
        P("pair"),
    )
    out_specs = P("pair", ("grow", "gcol"))
    return jax.shard_map(local, mesh=mesh, in_specs=in_specs, out_specs=out_specs, check_vma=False)
```

```python
import functools

import jax
import jax.numpy as jnp
from jax import lax
from jax.experimental import pallas as pl
from jax.experimental.pallas import tpu as pltpu
from jax.sharding import PartitionSpec as P

MESH = pl.DeviceIdType.MESH
TILE = 768
F32 = jnp.float32
BF16 = jnp.bfloat16
GROUP = 8
STATIC = 16


def units():
    found = []
    for high in range(STATIC // GROUP):
        for low in range(high + 1):
            for turn in range(GROUP // 2 + 1 if low == high else GROUP):
                found.append((high, low, turn, high != low or turn % (GROUP // 2) != 0))
    return found


def turned(block, turn):
    return block if turn % GROUP == 0 else pltpu.roll(block, turn % GROUP, 0)


def static_kernel(
        ngrow, ngcol, step, width_ref, panel_ref, table_ref, core_ref, left_ref, right_ref, proj_ref, back_ref, z_ref,
        y_ref, v_ref, mix_ref, amps_ref, widths, send_sem, high_sem, recv_sem, tree_send, tree_recv, own_sem, z_sem, in_sem):
    x, g, c = lax.axis_index("pair"), lax.axis_index("grow"), lax.axis_index("gcol")
    npair, depth, piece = panel_ref.shape
    half = depth // 2
    whole = npair * depth
    cols = core_ref.shape[1]
    steps = cols // step
    per = len(units()) * GROUP
    bits = ngrow.bit_length() - 1
    root = lax.div(c * ngrow, ngcol)
    first = lax.rem(c * ngrow, ngcol)

    def bit(value, b):
        return lax.rem(lax.div(value, 1 << b), 2)

    def flip(b):
        return g + (1 << b) * (1 - 2 * bit(g, b))

    differ = [lax.rem(bit(g, b) + bit(root, b), 2) for b in range(bits)]
    before = [jnp.int32(0)]
    for b in range(bits):
        before.append(before[-1] + differ[b])
    is_root = before[bits] == 0

    toward = lax.div(g * ngcol + ngrow - 1, ngrow)
    until = lax.div((g + 1) * ngcol - 1, ngrow)

    def order(t):
        both = jnp.minimum(c, ngcol - 1 - c)
        near = lax.div(t + 1, 2)
        inner = c + near * (1 - 2 * lax.rem(t, 2))
        outer = jnp.where(c < ngcol - 1 - c, c + t - both, c - t + both)
        return jnp.where(t <= 2 * both, inner, outer)

    def core_copy(t):
        rows = pl.ds(pl.multiple_of(order(t) * piece, 128), piece)
        return pltpu.make_async_copy(core_ref.at[rows, :], z_ref.at[rows, :], z_sem.at[t])

    def span(at):
        return pl.ds(pl.multiple_of(at * piece, 128), piece)

    brought = [
        pltpu.make_async_copy(panel_ref, left_ref.at[:, :, span(c)], in_sem.at[0]),
        pltpu.make_async_copy(table_ref, amps_ref, in_sem.at[1]),
        pltpu.make_async_copy(width_ref, widths, in_sem.at[2]),
    ]
    for copy in brought:
        copy.start()
    core_copy(0).start()

    barrier = pltpu.get_barrier_semaphore()

    def greet(device):
        pl.semaphore_signal(barrier, inc=1, device_id=device, device_id_type=MESH)

    expected = jnp.int32(0)
    for far in range(1, ngcol):
        for way in (0, 1):
            other = c + far * (1 - 2 * way)
            there = jnp.logical_and(other >= 0, other < ngcol)
            expected += jnp.where(there, 1, 0)

            @pl.when(there)
            def _(other=other):
                greet((x, g, other))

    for b in range(bits):
        expected += jnp.where(before[b] == 0, 1, 0)

        @pl.when(before[b] == 0)
        def _(b=b):
            greet((x, flip(b), c))

    def clear(i, carry):
        v_ref[pl.ds(pl.multiple_of(i * per, GROUP), per), :] = jnp.zeros((per, cols), F32)
        return carry

    lax.fori_loop(0, npair, clear, 0)
    def build(at):
        def one(p, carry):
            rows = left_ref[p, 0:STATIC, span(at)].astype(F32)
            block = [rows[GROUP * k : GROUP * (k + 1)] for k in range(STATIC // GROUP)]
            made = [block[high] * turned(block[low], -turn) for high, low, turn, _ in units()]
            for k in range(0, len(made), 2):
                both = jnp.concatenate(made[k : k + 2], axis=0).astype(BF16)
                y_ref[pl.ds(pl.multiple_of(p * per + GROUP * k, 16), 16), :] = both
            return carry

        lax.fori_loop(0, npair, one, 0)

    pl.semaphore_wait(barrier, expected)

    def spot(ref, h, at):
        return ref.at[:, h * half : (h + 1) * half, span(at)]

    def hop(h, at, far, way, own):
        return pltpu.make_async_remote_copy(
            src_ref=panel_ref.at[:, h * half : (h + 1) * half, :] if own else spot(left_ref, h, at), dst_ref=spot(left_ref, h, at),
            send_sem=send_sem.at[at, far - 1, way] if h == 0 else high_sem.at[far - 1, way], recv_sem=recv_sem.at[h, at],
            device_id=(x, g, c + far * (1 - 2 * way)), device_id_type=MESH)

    def branch(b, h, j, at):
        return pltpu.make_async_remote_copy(
            src_ref=spot(right_ref, h, j) if at is None else spot(left_ref, h, at), dst_ref=spot(right_ref, h, j),
            send_sem=tree_send.at[b, h, j], recv_sem=tree_recv.at[h, j],
            device_id=(x, flip(b), c), device_id_type=MESH)

    def own_right(h, j, at):
        return pltpu.make_async_copy(spot(left_ref, h, at), spot(right_ref, h, j), own_sem.at[h, j])

    def arrivals(s):
        return [(c - s, 0, c - s >= 0)] if s == 0 else [(c - s, 0, c - s >= 0), (c + s, 1, c + s <= ngcol - 1)]

    def inside(at):
        return jnp.logical_and(at >= first, at < first + ngrow)

    def onward(far, s, act):
        ways = [(c, 0, c >= 0), (c, 1, c >= 0)] if s == 0 else arrivals(s)
        for at, way, valid in ways:
            other = c + far * (1 - 2 * way)

            @pl.when(jnp.logical_and(valid, jnp.logical_and(other >= 0, other < ngcol)))
            def _(at=at, way=way):
                act(hop(0, at, far, way, s == 0))

    def upward(stage, act):
        for far in range(1, ngcol):
            for way in (0, 1):
                other = c + far * (1 - 2 * way)
                there = jnp.logical_and(other >= 0, other < ngcol)
                rooted = jnp.logical_and(other >= toward, other <= until)
                free = (c < 2 if way == 0 else c > ngcol - 3) if far == 1 else c < 0
                chosen = (rooted, jnp.logical_and(jnp.logical_not(rooted), free), jnp.logical_not(jnp.logical_or(rooted, free)), c >= 0)[stage]

                @pl.when(jnp.logical_and(there, chosen))
                def _(far=far, way=way):
                    act(hop(1, c, far, way, True))

    def start(copy):
        copy.start()

    def wait_send(copy):
        copy.wait_send()

    def to_tree(h, s):
        for at, _, valid in arrivals(s):
            @pl.when(jnp.logical_and(is_root, jnp.logical_and(valid, inside(at))))
            def _(at=at):
                for b in reversed(range(bits)):
                    branch(b, h, at - first, at).start()
                own_right(h, at - first, at).start()

    def lower(s):
        for at, _, valid in arrivals(s):
            @pl.when(valid)
            def _(at=at):
                hop(0, at, 1, 0, False).wait_recv()

        if s % 2 == 0:
            onward(1, s, start)
            onward(2, s, start)
        to_tree(0, s)
        if s == min(2, ngcol - 1):
            upward(2, start)

    def take_upper(s, root):
        for at, _, valid in arrivals(s):
            @pl.when(jnp.logical_and(valid, is_root if root else jnp.logical_not(is_root)))
            def _(at=at):
                hop(1, at, 1, 0, False).wait_recv()

    def upper(s):
        take_upper(s, True)
        to_tree(1, s)

    def tree(h, s):
        for at, _, valid in arrivals(s):
            here = jnp.logical_and(valid, inside(at))

            @pl.when(jnp.logical_and(is_root, here))
            def _(at=at):
                own_right(h, at - first, at).wait()

            @pl.when(jnp.logical_and(jnp.logical_not(is_root), here))
            def _(at=at):
                branch(0, h, at - first, None).wait_recv()
                for b in range(bits):
                    @pl.when(before[b + 1] == 0)
                    def _(b=b):
                        branch(b, h, at - first, None).start()

    onward(1, 0, start)
    onward(2, 0, start)
    upward(0, start)
    upward(1, start)

    for copy in brought:
        copy.wait()

    to_tree(0, 0)
    to_tree(1, 0)

    build(c)

    pick_row = lax.broadcasted_iota(jnp.int32, (depth, whole), 0)
    pick_col = lax.broadcasted_iota(jnp.int32, (depth, whole), 1)
    pick = jnp.where(lax.rem(pick_col, depth) == pick_row, 1.0, 0.0).astype(BF16)
    row = lax.broadcasted_iota(jnp.int32, (whole, whole), 0)
    col = lax.broadcasted_iota(jnp.int32, (whole, whole), 1)
    width = jnp.zeros((whole, whole), jnp.int32)
    for p in range(npair):
        width = jnp.where(lax.div(row, depth) == p, widths[p], width)
    keep = jnp.logical_and(lax.div(row, depth) == lax.div(col, depth), jnp.logical_and(lax.rem(row, depth) < width, lax.rem(col, depth) < width))
    spread = jnp.dot(amps_ref[...].reshape(whole, depth), pick, preferred_element_type=F32)
    mix_ref[...] = jnp.where(keep, spread, 0.0).astype(BF16)

    def low_tree(s):
        tree(0, s)

    def high_tree(s):
        tree(1, s)

    plan = {}
    end = (ngcol - 1) * steps

    def at_step(position, job, distance):
        plan.setdefault(position, []).append((job, distance))

    for t in range(1, ngcol):
        at_step(t * steps - (t > 1), lower, t)
    at_step(end - steps, low_tree, 0)
    at_step(end - steps, high_tree, 0)
    at_step(end - 1, low_tree, 1)
    for t in range(1, ngcol):
        at_step(end + (t - 2 if t > 2 else 2 * t - 5), upper, t)
    for t in range(1, ngcol):
        at_step(end + t, high_tree, t)
        if t > 1:
            at_step(end + t - 1, low_tree, t)

    def gain(i, t, s):
        wide = pl.ds(pl.multiple_of(s * step, 128), step)
        v_ref[:, wide] += jnp.dot(y_ref[...], z_ref[span(order(t)), wide], preferred_element_type=F32)

    def early(i, carry):
        t, s = lax.div(i, steps), lax.rem(i, steps)
        for when, jobs in plan.items():
            if when >= end:
                continue

            @pl.when(i == when)
            def _(jobs=jobs):
                for job, distance in jobs:
                    job(distance)

        for k in range(ngcol - 1):
            @pl.when(i == k * steps)
            def _(k=k):
                core_copy(k).wait()
                core_copy(k + 1).start()

        @pl.when(jnp.logical_and(s == 0, t > 0))
        def _():
            build(order(t))

        gain(i, t, s)
        return carry

    lax.fori_loop(0, (ngcol - 1) * steps, early, 0)

    last = ngcol - 1
    build(order(last))
    core_copy(last).wait()

    def fold(wide):
        def one(p, carry):
            proj = proj_ref[pl.ds(pl.multiple_of(p * depth, depth), STATIC), wide].astype(F32)
            block = [proj[GROUP * k : GROUP * (k + 1)] for k in range(STATIC // GROUP)]
            total = [None] * len(block)
            for k, (high, low, turn, both) in enumerate(units()):
                v = v_ref[pl.ds(pl.multiple_of(p * per, GROUP) + GROUP * k, GROUP), wide]
                straight = v * turned(block[low], -turn)
                total[high] = straight if total[high] is None else total[high] + straight
                if both:
                    cross = turned(v * block[high], turn)
                    total[low] = cross if total[low] is None else total[low] + cross
            for k, value in enumerate(total):
                back_ref[pl.ds(pl.multiple_of(p * STATIC, STATIC) + GROUP * k, GROUP), wide] = value
            return carry

        lax.fori_loop(0, npair, one, 0)

    fine = 256 if piece % 256 == 0 else 128

    def late(k, carry):
        at = order(k)
        for when, jobs in plan.items():
            if when < end:
                continue

            @pl.when(k == when - end)
            def _(jobs=jobs):
                for job, distance in jobs:
                    job(distance)

        @pl.when(inside(at))
        def _():
            here = span(at - first)
            right = right_ref[:, :, here].reshape(whole, piece)
            proj_ref[:, here] = jnp.dot(mix_ref[...], right, preferred_element_type=F32).astype(BF16)
            v_ref[:, here] += jnp.dot(y_ref[...], z_ref[span(order(last)), here], preferred_element_type=F32)

            def part(n, carry):
                fold(pl.ds(pl.multiple_of((at - first) * piece + n * fine, 128), fine))
                return carry

            lax.fori_loop(0, piece // fine, part, 0)

        return carry

    lax.fori_loop(0, ngcol, late, 0)
    for s in range(1, ngcol):
        take_upper(s, False)

    upward(3, wait_send)
    for s in range(0, ngcol, 2):
        onward(1, s, wait_send)
        onward(2, s, wait_send)
    for s in range(ngcol):
        for at, _, valid in arrivals(s):
            here = jnp.logical_and(valid, inside(at))
            for h in (0, 1):
                for b in range(bits):
                    @pl.when(jnp.logical_and(before[b + 1] == 0, here))
                    def _(at=at, b=b, h=h):
                        branch(b, h, at - first, None).wait_send()


def static_part(panels, amplitudes, widths, core_matrix, ngrow, ngcol):
    npair, depth, piece = panels.shape
    rows, cols = core_matrix.shape
    step = TILE if cols % TILE == 0 else piece
    made = npair * len(units()) * GROUP
    bits = ngrow.bit_length() - 1
    vmem = pl.BlockSpec(memory_space=pltpu.VMEM)
    return pl.pallas_call(
        functools.partial(static_kernel, ngrow, ngcol, step),
        out_shape=(
            jax.ShapeDtypeStruct((npair, depth, rows), BF16),
            jax.ShapeDtypeStruct((npair, depth, cols), BF16),
            jax.ShapeDtypeStruct((npair * depth, cols), BF16),
            jax.ShapeDtypeStruct((npair * STATIC, cols), F32),
            jax.ShapeDtypeStruct((rows, cols), BF16),
        ),
        in_specs=[pl.BlockSpec(memory_space=pltpu.HBM)] * 4,
        out_specs=[vmem] * 5,
        scratch_shapes=[
            pltpu.VMEM((made, piece), BF16),
            pltpu.VMEM((made, cols), F32),
            pltpu.VMEM((npair * depth, npair * depth), BF16),
            pltpu.VMEM(amplitudes.shape, BF16),
            pltpu.SMEM(widths.shape, jnp.int32),
            pltpu.SemaphoreType.DMA((ngcol, 2, 2)),
            pltpu.SemaphoreType.DMA((ngcol - 1, 2)),
            pltpu.SemaphoreType.DMA((2, ngcol)),
            pltpu.SemaphoreType.DMA((bits, 2, ngrow)),
            pltpu.SemaphoreType.DMA((2, ngrow)),
            pltpu.SemaphoreType.DMA((2, ngrow)),
            pltpu.SemaphoreType.DMA((ngcol,)),
            pltpu.SemaphoreType.DMA((3,)),
        ],
        compiler_params=pltpu.CompilerParams(collective_id=0, has_side_effects=True, vmem_limit_bytes=22 << 20),
        name="static_part",
    )(widths, panels, amplitudes, core_matrix)


def rest_kernel(widths, left_ref, right_ref, proj_ref, back_ref, z_ref, out_ref, y_ref, x_ref, v_ref, p_ref, g_ref, sum_ref, lad_ref):
    npair, depth, rows = left_ref.shape
    cols = z_ref.shape[1]
    tile = v_ref.shape[1]
    whole = npair * depth
    groups = depth // GROUP
    skip = STATIC // GROUP

    def duos(p):
        return lax.div(widths[p] + 1, 2)

    def rows_in(p):
        count = duos(p)
        found = jnp.int32(0)
        for group in range(skip, groups):
            found += 16 * (group + 1) * jnp.clip(count - 4 * group, 0, 4)
        return found

    def each_duo(p, offset, body):
        count = duos(p)
        for group in range(skip, groups):
            low = 4 * group
            begin = offset

            def run(duo, carry, group=group, low=low, begin=begin):
                body(group, 2 * duo, pl.multiple_of(begin + 16 * (group + 1) * (duo - low), 16))
                return carry

            lax.fori_loop(low, jnp.clip(count, low, low + 4), run, 0)
            offset = offset + 16 * (group + 1) * jnp.clip(count - low, 0, 4)

    def build(p, offset):
        x_ref[...] = left_ref[p].astype(F32)

        def duo(group, a, base):
            first, second = x_ref[pl.ds(a, 1), :], x_ref[pl.ds(a + 1, 1), :]
            for other in range(group + 1):
                block = x_ref[GROUP * other : GROUP * (other + 1), :]
                both = jnp.concatenate([first * block, second * block], axis=0)
                y_ref[pl.ds(base + 16 * other, 16), :] = both.astype(BF16)

        each_duo(p, offset, duo)
        return offset + rows_in(p)

    total = lax.fori_loop(0, npair, build, jnp.int32(0))
    sum_ref[...] = jnp.zeros_like(sum_ref)
    size, grain = 512, 64
    full = jnp.where(total > 0, lax.div(jnp.maximum(total - size // 2 - 1, 0), size), 0)
    left_over = total - full * size

    def column(j, carry):
        lanes = pl.ds(pl.multiple_of(j * tile, 128), tile)

        def multiply(base, count):
            at = pl.ds(base if isinstance(base, int) else pl.multiple_of(base, grain), count)
            v_ref[at, :] = jnp.dot(y_ref[at, :], z_ref[:, lanes], preferred_element_type=F32)

        def block(i, carry):
            multiply(i * size, size)
            return carry

        lax.fori_loop(0, full, block, 0)
        for count in range(grain, size + size // 2 + 1, grain):
            @pl.when(jnp.logical_and(left_over > count - grain, left_over <= count))
            def _(count=count):
                multiply(full * size, count)

        def fold(p, offset):
            mine = pl.ds(pl.multiple_of(p * depth, depth), depth)
            low = pl.ds(pl.multiple_of(p * depth, depth), STATIC)
            high = pl.ds(pl.multiple_of(p * depth, depth) + STATIC, depth - STATIC)
            p_ref[...] = proj_ref[mine, lanes].astype(F32)
            g_ref[low, :] = back_ref[pl.ds(pl.multiple_of(p * STATIC, STATIC), STATIC), lanes]
            g_ref[high, :] = jnp.zeros((depth - STATIC, tile), F32)
            origin = p * depth

            def duo(group, a, base):
                first, second = p_ref[pl.ds(a, 1), :], p_ref[pl.ds(a + 1, 1), :]
                sum0 = sum1 = None
                for other in range(group + 1):
                    upper = v_ref[pl.ds(base + 16 * other, 8), :]
                    lower = v_ref[pl.ds(base + 16 * other + 8, 8), :]
                    proj = p_ref[GROUP * other : GROUP * (other + 1), :]
                    sum0 = upper * proj if sum0 is None else sum0 + upper * proj
                    sum1 = lower * proj if sum1 is None else sum1 + lower * proj
                    if other < group:
                        g_ref[pl.ds(pl.multiple_of(origin, depth) + GROUP * other, GROUP), :] += upper * first + lower * second
                g_ref[pl.ds(origin + a, 1), :] += jnp.sum(sum0, axis=0, keepdims=True)
                g_ref[pl.ds(origin + a + 1, 1), :] += jnp.sum(sum1, axis=0, keepdims=True)

            each_duo(p, offset, duo)
            return offset + rows_in(p)

        lax.fori_loop(0, npair, fold, jnp.int32(0))
        sum_ref[...] += lax.dot_general(
            g_ref[...].astype(BF16), right_ref[:, :, lanes].reshape(whole, tile), (((1,), (1,)), ((), ())), preferred_element_type=F32)
        return carry

    lax.fori_loop(0, cols // tile, column, 0)

    out_ref[...] = jnp.zeros_like(out_ref)
    ngrow, ngcol, padded, lanes = out_ref.shape
    share = depth // (ngrow * ngcol)
    for p in range(npair):
        width = widths[p]
        live = jnp.logical_and(
            lax.broadcasted_iota(jnp.int32, (depth, depth), 0) < width,
            lax.broadcasted_iota(jnp.int32, (depth, depth), 1) < width)
        lad_ref[...] = jnp.where(live, sum_ref[depth * p : depth * (p + 1), depth * p : depth * (p + 1)], 0.0)
        parts = [lad_ref[pl.ds(r, ngrow * ngcol, stride=share), :] for r in range(share)]
        row = parts[0] if share == 1 else jnp.concatenate(parts, axis=1)
        for at in range(ngrow):
            out_ref[at, :, p, 0 : share * depth] = row[at * ngcol : (at + 1) * ngcol]


def rest(left, right, proj, back, core, widths, ngrow, ngcol):
    npair, depth, rows = left.shape
    cols = core.shape[1]
    tile = TILE if cols % TILE == 0 else cols // 2
    most = npair * sum(16 * (group + 1) * 4 for group in range(STATIC // GROUP, depth // GROUP))
    most = -(-most // 128) * 128
    padded = -(-npair // 8) * 8
    vmem = pl.BlockSpec(memory_space=pltpu.VMEM)
    return pl.pallas_call(
        rest_kernel,
        out_shape=jax.ShapeDtypeStruct((ngrow, ngcol, padded, 128), F32),
        in_specs=[pl.BlockSpec(memory_space=pltpu.SMEM)] + [vmem] * 5,
        out_specs=vmem,
        scratch_shapes=[
            pltpu.VMEM((most, rows), BF16),
            pltpu.VMEM((depth, rows), F32),
            pltpu.VMEM((most, tile), F32),
            pltpu.VMEM((depth, tile), F32),
            pltpu.VMEM((npair * depth, tile), F32),
            pltpu.VMEM((npair * depth, npair * depth), F32),
            pltpu.VMEM((depth, depth), F32),
        ],
        compiler_params=pltpu.CompilerParams(vmem_limit_bytes=30 << 20),
        name="rest",
    )(widths, left, right, proj, back, core)


def settle_kernel(npart, ngrow, ngcol, npair, plan_ref, lad_ref, out_ref, row_ref, sum_ref, held_ref, send_sem, recv_sem, wide_send, wide_recv):
    x, g, c = lax.axis_index("pair"), lax.axis_index("grow"), lax.axis_index("gcol")
    count = npart * ngrow
    me = x * ngrow + g

    def seat(k):
        other = lax.rem(me + k, count)
        return other, lax.div(other, ngrow), lax.rem(other, ngrow)

    barrier = pltpu.get_barrier_semaphore()

    def greet(device):
        pl.semaphore_signal(barrier, inc=1, device_id=device, device_id_type=MESH)

    for k in range(1, ngcol):
        greet((x, g, lax.rem(c + k, ngcol)))
    for k in range(1, count):
        _, xo, go = seat(k)
        greet((xo, go, c))
    pl.semaphore_wait(barrier, ngcol - 1 + count - 1)

    def near(k, at):
        to = lax.rem(c + k, ngcol)
        return pltpu.make_async_remote_copy(
            src_ref=lad_ref.at[:, to], dst_ref=row_ref.at[at], send_sem=send_sem.at[k], recv_sem=recv_sem.at[at],
            device_id=(x, g, to), device_id_type=MESH)

    def wide(k, at):
        _, xo, go = seat(k)
        return pltpu.make_async_remote_copy(
            src_ref=sum_ref.at[go], dst_ref=held_ref.at[at], send_sem=wide_send.at[k], recv_sem=wide_recv.at[at],
            device_id=(xo, go, c), device_id_type=MESH)

    for k in range(1, ngcol):
        near(k, c).start()
    total = lad_ref[:, c]
    for k in range(1, ngcol):
        source = lax.rem(c + k, ngcol)
        near(k, source).wait_recv()
        total = total + row_ref[source]
    sum_ref[...] = total
    for k in range(1, count):
        wide(k, me).start()
    held_ref[me] = sum_ref[g]
    for k in range(1, count):
        wide(k, seat(k)[0]).wait_recv()
    slots = out_ref.shape[0]
    done = [jnp.zeros(out_ref.shape[1:], F32) for _ in range(slots)]
    for part in range(npart):
        summed = jnp.sum(held_ref[part * ngrow : (part + 1) * ngrow], axis=0)
        for p in range(npair):
            for s in range(slots):
                done[s] = jnp.where(plan_ref[s] == part * npair + p, summed[p], done[s])
    for s in range(slots):
        out_ref[s] = done[s]
    for k in range(1, ngcol):
        near(k, c).wait_send()
    for k in range(1, count):
        wide(k, me).wait_send()


def settle(lad, plan, mesh_shape):
    npart, ngrow, ngcol = mesh_shape
    count = npart * ngrow
    _, _, padded, lanes = lad.shape
    npair = plan.shape[0]
    return pl.pallas_call(
        functools.partial(settle_kernel, npart, ngrow, ngcol, npair),
        out_shape=jax.ShapeDtypeStruct((npair, lanes), F32),
        in_specs=[pl.BlockSpec(memory_space=pltpu.SMEM), pl.BlockSpec(memory_space=pltpu.VMEM)],
        out_specs=pl.BlockSpec(memory_space=pltpu.VMEM),
        scratch_shapes=[
            pltpu.VMEM((ngcol, ngrow, padded, lanes), F32),
            pltpu.VMEM((ngrow, padded, lanes), F32),
            pltpu.VMEM((count, padded, lanes), F32),
            pltpu.SemaphoreType.DMA((ngcol,)),
            pltpu.SemaphoreType.DMA((ngcol,)),
            pltpu.SemaphoreType.DMA((count,)),
            pltpu.SemaphoreType.DMA((count,)),
        ],
        compiler_params=pltpu.CompilerParams(collective_id=1, has_side_effects=True, vmem_limit_bytes=8 << 20),
        name="settle",
    )(plan, lad)


def solution(mesh):
    shape = (mesh.shape["pair"], mesh.shape["grow"], mesh.shape["gcol"])

    def local(core_matrix, pair_panels, amplitudes, pair_widths, batch_plan):
        pinned = [pltpu.with_memory_space_constraint(array, pltpu.HBM) for array in (pair_panels, amplitudes, pair_widths, core_matrix)]
        left, right, proj, back, core = static_part(*pinned, shape[1], shape[2])
        lad = rest(left, right, proj, back, core, pair_widths, shape[1], shape[2])
        width = amplitudes.shape[1] ** 2 // (shape[1] * shape[2])
        return settle(lad, batch_plan, shape)[:, :width]

    in_specs = (
        P("grow", "gcol"),
        P("pair", None, ("grow", "gcol")),
        P("pair", None, None),
        P("pair"),
        P("pair"),
    )
    out_specs = P("pair", ("grow", "gcol"))
    return jax.shard_map(local, mesh=mesh, in_specs=in_specs, out_specs=out_specs, check_vma=False)
```
